32 devices in a mesh: blk: 8 (over z, x), mp: 4 (over y, core).
Axes of the slice: x: 2, y: 2, z: 4, core: 2. Of those that a mesh axis runs over, the one named last changes fastest.
Arguments:
- lengths: int32 [4], replicated, may hold values from 1 to 512, 1024 in all
- groups: int32 [4], replicated, may hold values from 0 to 3, as said below
- deal: int32 [1024], P('blk'), may hold values from 0 to 1023, as said below
- prefix_block: int32 [8], P('blk'), may hold values from 0 to 7, each once
- queries: bfloat16 [1024, 2048], P('blk', 'mp'), may hold values from -8 to 8
- keys: bfloat16 [1024, 512], P('blk', 'mp'), may hold values from -8 to 8
- values: bfloat16 [1024, 512], P('blk', 'mp'), may hold values from -6 to 6
- prefix_key_blocks: bfloat16 [512, 512], P('blk', 'mp'), may hold values from -8 to 8
- prefix_value_blocks: bfloat16 [512, 512], P('blk', 'mp'), may hold values from -6 to 6
- out_weight: bfloat16 [2048, 4096], P('mp'), may hold values from -0.125 to 0.125
Outputs:
- layer_out: bfloat16 [1024, 4096], P('blk', 'mp')
The draws below stay inside these ranges and needn't reach their ends.
Inputs may be any that keep to these rules, and one draw needn't show every extreme that they name: The 4 lengths sum to 1024; the largest is 512. `groups`: each group has exactly 1 request. `deal`: a permutation of the request-order rows; on every index of blk, the 16 slots c * 16 to c * 16 + 15 hold rows taken from request-order rows c * 128 to c * 128 + 127, and over all indices of blk each of those rows appears once. `prefix_block`: a permutation of the blocks.
All inputs are finite; a program needn't handle non-finite values.
Results may differ from the reference program's by a relative error of at most 0.012.
Values may be sent and summed in bfloat16 or wider, within the bound.
A program may use at most 64 MiB of HBM per device.

```python
import math
import jax
import jax.numpy as jnp
import numpy as np
from jax import lax

D = 4096
QUERY_HEADS = 16
KEY_VALUE_HEADS = 4
HEAD_WIDTH = 128
GROUPS = 4
TOK_DEV = 128
BLOCK_PREFIX_LEN = 64
PREFIX_BLOCKS = 8
SUFFIX_TOKENS = 1024
REQS = 4
LONGEST = 512


def draw_groups(key, part):
    shuffled = jax.random.permutation(jax.random.fold_in(key, 11), REQS)
    return (shuffled % GROUPS).astype(jnp.int32)


def draw_deal(key, part):
    piece_rows = TOK_DEV // PREFIX_BLOCKS
    base_key = jax.random.fold_in(key, 23)

    def shuffle_one(source_index):
        return jax.random.permutation(jax.random.fold_in(base_key, source_index), TOK_DEV)
    shuffles = jax.vmap(shuffle_one)(jnp.arange(PREFIX_BLOCKS))
    row_ids = shuffles.reshape(PREFIX_BLOCKS, PREFIX_BLOCKS, piece_rows) + (jnp.arange(PREFIX_BLOCKS) * TOK_DEV)[:, None, None]
    return jnp.transpose(row_ids, (1, 0, 2)).reshape(SUFFIX_TOKENS).astype(jnp.int32)


def draw_queries(key, part):
    array_shape = (SUFFIX_TOKENS, QUERY_HEADS * HEAD_WIDTH)
    sub_key = jax.random.fold_in(key, 37)
    drawn = jnp.clip(1.7 * jax.random.normal(sub_key, array_shape, jnp.float32), -8.0, 8.0)
    return drawn.astype(jnp.bfloat16)


def draw_prefix_key_blocks(key, part):
    array_shape = (PREFIX_BLOCKS * BLOCK_PREFIX_LEN, KEY_VALUE_HEADS * HEAD_WIDTH)
    sub_key = jax.random.fold_in(key, 41)
    drawn = jnp.clip(1.7 * jax.random.normal(sub_key, array_shape, jnp.float32), -8.0, 8.0)
    return drawn.astype(jnp.bfloat16)


def block_scale(key, shape, shards, low, top_value):
    loudness = 1.0
    for dim, shards_of in shards:
        draws = jax.random.uniform(jax.random.fold_in(jax.random.fold_in(key, 6), dim), (shards_of,), jnp.float32, low / len(shards), top_value / len(shards))
        loudness = loudness * jnp.repeat(jnp.exp(draws), shape[dim] // shards_of).reshape((-1,) + (1,) * (len(shape) - 1 - dim))
    return loudness


def profile(amount, total, limit, skew):
    loads = [(1 << 20) // math.isqrt(rank ** skew) + 1 for rank in range(2, amount + 1)]
    surplus, given = total - limit - (amount - 1), [1] * (amount - 1)
    while surplus > 0:
        movable = [i for i in range(amount - 1) if given[i] < limit]
        mass, left = sum([loads[i] for i in movable]), surplus
        for i in movable:
            more = min(limit - given[i], max(1, left * loads[i] // mass), surplus)
            given[i] = given[i] + more
            surplus = surplus - more
    return np.array([limit] + given)


def uneven(key, count, total, limit, slope):
    if count == 2:
        one = jax.random.randint(key, (), max(1, total - limit), min(limit, total - 1) + 1)
        return jnp.stack([one, total - one])
    sizes = jnp.asarray(profile(count, total, limit, slope), jnp.int32)
    pairs = (count - 1) // 2
    source_of, taker = sizes[1:1 + 2 * pairs:2], sizes[2:2 + 2 * pairs:2]
    slack = jnp.minimum(source_of - 1, limit - taker)
    passed = jax.random.randint(jax.random.fold_in(key, 1), (pairs,), 0, 1 << 20) % (slack + 1)
    sizes = sizes.at[1:1 + 2 * pairs:2].set(source_of - passed).at[2:2 + 2 * pairs:2].set(taker + passed)
    return sizes[jax.random.permutation(jax.random.fold_in(key, 2), count)]


def bell_draw(stream_key, dims, width, reach, cuts=(), kind=jnp.bfloat16):
    entries = width * jax.random.normal(stream_key, dims, jnp.float32)
    if cuts:
        entries = entries * block_scale(stream_key, dims, cuts, -0.22, 0.18)
    return jnp.clip(entries, -reach, reach).astype(kind)


def setup_inputs(seed: int = 0) -> dict:
    seeds = jax.random.split(jax.random.key(seed), 11)
    return {
        "lengths": uneven(seeds[0], REQS, SUFFIX_TOKENS, LONGEST, 2).astype(jnp.int32),
        "groups": draw_groups(jax.random.fold_in(seeds[10], 71), 0),
        "deal": draw_deal(jax.random.fold_in(seeds[10], 71), 0),
        "prefix_block": jax.random.permutation(seeds[3], PREFIX_BLOCKS).astype(jnp.int32),
        "queries": draw_queries(jax.random.fold_in(seeds[10], 71), 0),
        "keys": bell_draw(seeds[5], (SUFFIX_TOKENS, KEY_VALUE_HEADS * HEAD_WIDTH), 1.7, 8.0, ((0, 8), (1, 4))),
        "values": bell_draw(seeds[6], (SUFFIX_TOKENS, KEY_VALUE_HEADS * HEAD_WIDTH), 1.0, 6.0, ((0, 8), (1, 4))),
        "prefix_key_blocks": draw_prefix_key_blocks(jax.random.fold_in(seeds[10], 71), 0),
        "prefix_value_blocks": bell_draw(seeds[8], (PREFIX_BLOCKS * BLOCK_PREFIX_LEN, KEY_VALUE_HEADS * HEAD_WIDTH), 1.0, 6.0, ((0, 8), (1, 4))),
        "out_weight": bell_draw(seeds[9], (QUERY_HEADS * HEAD_WIDTH, D), (QUERY_HEADS * HEAD_WIDTH) ** -0.5, 0.125, ((0, 4),)),
    }


NEGATIVE = -1e+30

def request_of(row_ids, req_ends):
    return lax.optimization_barrier(jnp.sum((row_ids[:, None] >= req_ends[None, :]).astype(jnp.int32), axis=1)).astype(jnp.int32)

def reference(lengths, groups, deal, prefix_block, queries, keys, values, prefix_key_blocks, prefix_value_blocks, out_weight):
    sorted_queries = jnp.zeros_like(queries).at[deal].set(queries)
    sorted_keys = jnp.zeros_like(keys).at[deal].set(keys)
    sorted_values = jnp.zeros_like(values).at[deal].set(values)
    req_ends = jnp.cumsum(lengths).astype(jnp.int32)
    row_ids = jnp.arange(SUFFIX_TOKENS, dtype=jnp.int32)
    row_req = request_of(row_ids, req_ends)
    row_group = groups[row_req].astype(jnp.int32)
    key_group = (jnp.repeat(prefix_block, BLOCK_PREFIX_LEN) // (PREFIX_BLOCKS // GROUPS)).astype(jnp.int32)
    query_per_key_head = QUERY_HEADS // KEY_VALUE_HEADS
    stored_keys = prefix_key_blocks.astype(jnp.float32).reshape(-1, KEY_VALUE_HEADS, HEAD_WIDTH)
    stored_values = prefix_value_blocks.astype(jnp.float32).reshape(-1, KEY_VALUE_HEADS, HEAD_WIDTH)
    stretch_keys = min(LONGEST + 512, SUFFIX_TOKENS)
    score_scale = 1.0 / math.sqrt(HEAD_WIDTH)

    def one_block(block_index):
        row_begin = (block_index * 512).astype(jnp.int32)
        key_begin = jnp.clip(row_begin + 512 - stretch_keys, 0, SUFFIX_TOKENS - stretch_keys).astype(jnp.int32)
        query_float = lax.dynamic_slice_in_dim(sorted_queries, row_begin, 512, 0).astype(jnp.float32).reshape(512, KEY_VALUE_HEADS, query_per_key_head, HEAD_WIDTH)
        suffix_key_rows = lax.dynamic_slice_in_dim(sorted_keys, key_begin, stretch_keys, 0).astype(jnp.float32).reshape(stretch_keys, KEY_VALUE_HEADS, HEAD_WIDTH)
        suffix_value_rows = lax.dynamic_slice_in_dim(sorted_values, key_begin, stretch_keys, 0).astype(jnp.float32).reshape(stretch_keys, KEY_VALUE_HEADS, HEAD_WIDTH)
        query_rows = row_begin + jnp.arange(512, dtype=jnp.int32)
        key_rows = key_begin + jnp.arange(stretch_keys, dtype=jnp.int32)
        query_req = lax.dynamic_slice_in_dim(row_req, row_begin, 512, 0)
        query_group = lax.dynamic_slice_in_dim(row_group, row_begin, 512, 0)
        key_req = lax.dynamic_slice_in_dim(row_req, key_begin, stretch_keys, 0)
        own_mask = (key_req[None, :] == query_req[:, None]) & (key_rows[None, :] <= query_rows[:, None])
        cache_mask = key_group[None, :] == query_group[:, None]
        all_keys = jnp.concatenate([stored_keys, suffix_key_rows], axis=0)
        all_values = jnp.concatenate([stored_values, suffix_value_rows], axis=0)
        visible = jnp.concatenate([cache_mask, own_mask], axis=1)[:, None, None, :]
        scores = jnp.einsum('qgjd,ngd->qgjn', query_float, all_keys) * score_scale
        scores = jnp.where(visible, scores, NEGATIVE)
        row_top = lax.optimization_barrier(jnp.max(scores, axis=3, keepdims=True))
        weights = jnp.where(visible, jnp.exp(scores - row_top), 0.0)
        total = lax.optimization_barrier(jnp.sum(weights, axis=3))
        rounded = lax.optimization_barrier(weights.astype(jnp.bfloat16))
        mixed = jnp.einsum('qgjn,ngd->qgjd', rounded.astype(jnp.float32), all_values)
        return (mixed / total[..., None]).reshape(512, QUERY_HEADS * HEAD_WIDTH).astype(jnp.bfloat16)
    attended = lax.map(one_block, jnp.arange(SUFFIX_TOKENS // 512)).reshape(SUFFIX_TOKENS, QUERY_HEADS * HEAD_WIDTH)
    return jnp.dot(attended, out_weight, preferred_element_type=jnp.float32).astype(jnp.bfloat16)
```

```python
import functools
import math

import jax
import jax.numpy as jnp
from jax import lax
from jax.experimental import pallas as pl
from jax.experimental.pallas import tpu as pltpu
from jax.sharding import PartitionSpec as P

HEAD_WIDTH = 128
GROUPS = 4


NEGATIVE = -1e30


def request_index(row_ids, req_ends):
    return jnp.sum((row_ids[:, None] >= req_ends[None, :]).astype(jnp.int32), axis=1)


def lookup(values_table, indices):
    slots = jnp.arange(values_table.shape[0], dtype=jnp.int32)
    return jnp.sum(jnp.where(indices[:, None] == slots[None, :], values_table[None, :], 0), axis=1)


def attend(flash_state, grouped, key_block, value_block, visible):
    run_best, run_total, run_accum = flash_state
    key_count = key_block.shape[0]
    kv_heads = grouped.shape[1]
    head_size = grouped.shape[3]
    score_scale = 1.0 / math.sqrt(head_size)
    keys_three = key_block.reshape(key_count, kv_heads, head_size)
    values_three = value_block.reshape(key_count, kv_heads, head_size)
    scores = (
        jnp.einsum("rgjd,ngd->rgjn", grouped, keys_three, preferred_element_type=jnp.float32)
        * score_scale
    )
    shown = visible[:, None, None, :]
    scores = jnp.where(shown, scores, NEGATIVE)
    new_best = jnp.maximum(run_best, jnp.max(scores, axis=3))
    weights = jnp.where(shown, jnp.exp(scores - new_best[..., None]), 0.0)
    factor = jnp.exp(run_best - new_best)
    run_total = run_total * factor + jnp.sum(weights, axis=3)
    mixed = jnp.einsum(
        "rgjn,ngd->rgjd",
        weights.astype(jnp.bfloat16),
        values_three,
        preferred_element_type=jnp.float32,
    )
    run_accum = run_accum * factor[..., None] + mixed
    return (new_best, run_total, run_accum)


def sweep(flash_state, grouped, key_block, value_block, key_info, visible_of):
    key_count = key_block.shape[0]
    step_width = key_count if key_count <= 1024 else math.gcd(key_count, 512)
    if step_width == key_count:
        return attend(flash_state, grouped, key_block, value_block, visible_of(key_info))

    def one_step(carried, step_index):
        offset = step_index * step_width
        key_part = lax.dynamic_slice_in_dim(key_block, offset, step_width, 0)
        value_part = lax.dynamic_slice_in_dim(value_block, offset, step_width, 0)
        info_part = lax.dynamic_slice_in_dim(key_info, offset, step_width, 0)
        return (attend(carried, grouped, key_part, value_part, visible_of(info_part)), None)

    flash_state, _ = lax.scan(
        one_step, flash_state, jnp.arange(key_count // step_width, dtype=jnp.int32)
    )
    return flash_state


def plain_shards(
    lengths,
    groups,
    deal,
    prefix_block,
    queries,
    keys,
    values,
    prefix_key_blocks,
    prefix_value_blocks,
    out_weight,
):
    count_rows = queries.shape[0]
    kv_heads = keys.shape[1] // HEAD_WIDTH
    query_per_key_head = queries.shape[1] // keys.shape[1]
    devices = lax.axis_size("blk")
    my_index = lax.axis_index("blk")
    piece_rows = count_rows // devices
    per_group = devices // GROUPS
    prefix_rows = prefix_key_blocks.shape[0]
    req_ends = jnp.cumsum(lengths)
    arrived = lax.all_to_all(
        deal.reshape(devices, piece_rows), "blk", split_axis=0, concat_axis=0, tiled=True
    )
    placed = arrived.reshape(count_rows) - my_index * count_rows

    def prefix_pass(flash_state, grouped, query_group, block_ids):

        def prefix_step(carried, kv_piece):
            key_count = kv_piece[0].shape[0]
            owners = jnp.arange(key_count, dtype=jnp.int32) // prefix_rows
            key_group = jnp.take(block_ids, owners) // per_group

            def same_group(key_info):
                return key_info[None, :] == query_group[:, None]

            return sweep(carried, grouped, kv_piece[0], kv_piece[1], key_group, same_group)

        return prefix_step(
            flash_state,
            (
                lax.all_gather(prefix_key_blocks, "blk", axis=0, tiled=True),
                lax.all_gather(prefix_value_blocks, "blk", axis=0, tiled=True),
            ),
        )

    def suffix_rule(query_rows, query_req):

        def same_request(key_info):
            key_req = request_index(key_info, req_ends)
            return (
                (key_info[None, :] >= 0)
                & (key_req[None, :] == query_req[:, None])
                & (key_info[None, :] <= query_rows[:, None])
            )

        return same_request

    key_rows, block_ids = (
        lax.all_gather(deal, "blk", axis=0, tiled=True),
        lax.all_gather(prefix_block, "blk", axis=0, tiled=True),
    )
    query_rows = deal
    query_req = request_index(query_rows, req_ends)
    query_group = lookup(groups, query_req)
    grouped = queries.reshape(count_rows, kv_heads, query_per_key_head, HEAD_WIDTH)
    flash_state = prefix_pass(
        (
            jnp.full((count_rows, kv_heads, query_per_key_head), NEGATIVE, jnp.float32),
            jnp.zeros((count_rows, kv_heads, query_per_key_head), jnp.float32),
            jnp.zeros((count_rows, kv_heads, query_per_key_head, HEAD_WIDTH), jnp.float32),
        ),
        grouped,
        query_group,
        block_ids,
    )
    visible_of = suffix_rule(query_rows, query_req)
    kv_piece = (
        lax.all_gather(keys, "blk", axis=0, tiled=True),
        lax.all_gather(values, "blk", axis=0, tiled=True),
    )
    key_info = key_rows
    flash_state = sweep(flash_state, grouped, kv_piece[0], kv_piece[1], key_info, visible_of)
    run_best, run_total, run_accum = flash_state
    attended = (run_accum / run_total[..., None]).astype(jnp.bfloat16).reshape(count_rows, -1)
    returned = lax.all_to_all(
        attended.reshape(devices, piece_rows, -1), "blk", split_axis=0, concat_axis=0, tiled=True
    )
    flat = returned.reshape(count_rows, returned.shape[2])
    ordered = jnp.zeros_like(flat).at[placed].set(flat)
    partial_value = jnp.dot(ordered, out_weight, preferred_element_type=jnp.float32)
    return lax.psum_scatter(
        partial_value.astype(jnp.bfloat16), "mp", scatter_dimension=1, tiled=True
    )


LOG2E = 1.4426950408889634


def fused_kernel(
    devices,
    lengths_ref,
    groups_ref,
    block_ref,
    deal_ref,
    q_hbm,
    k_hbm,
    v_hbm,
    pk_hbm,
    pv_hbm,
    w_hbm,
    out_ref,
    q_buf,
    k_buf,
    v_buf,
    pk_buf,
    pv_buf,
    w_buf,
    meta_buf,
    score_buf,
    weight_buf,
    top_buf,
    bias_buf,
    att_buf,
    ret_buf,
    send_a,
    recv_a,
    send_b,
    recv_b,
    send_c,
    recv_c,
    part_buf,
    local_sem,
    own_sem,
    w_sem,
    gather_send,
    gather_recv,
    a2a_send,
    a2a_recv,
    red_send,
    red_recv,
):
    n = devices
    me = lax.axis_index("blk")
    m = lax.axis_index("mp")
    y = m // 2
    c = m - y * 2
    sibling = y * 2 + (1 - c)
    across = (1 - y) * 2 + c
    rows = q_buf.shape[0]
    heads = q_buf.shape[1] // HEAD_WIDTH
    piece = rows // n
    requests = lengths_ref.shape[0]
    per_group = n // GROUPS
    width = out_ref.shape[1]
    peers = [lax.rem(me + k, n) for k in range(n)]
    MESH = pl.DeviceIdType.MESH

    meta_buf[0] = jnp.zeros(meta_buf.shape[1:], jnp.int32)
    meta_buf[0, 0:1, :] = deal_ref[...]
    meta_buf[0, 1:2, :] = jnp.full((1, rows), block_ref[0] // per_group, jnp.int32)

    barrier = pltpu.get_barrier_semaphore()
    for k in range(1, n):
        pl.semaphore_signal(barrier, inc=1, device_id={"blk": peers[k]}, device_id_type=MESH)
    pl.semaphore_signal(barrier, inc=1, device_id={"mp": sibling}, device_id_type=MESH)
    pl.semaphore_signal(barrier, inc=1, device_id={"mp": across}, device_id_type=MESH)

    local = [
        pltpu.make_async_copy(q_hbm, q_buf, local_sem.at[0]),
        pltpu.make_async_copy(k_hbm, k_buf.at[0], local_sem.at[1]),
        pltpu.make_async_copy(v_hbm, v_buf.at[0], local_sem.at[2]),
        pltpu.make_async_copy(pk_hbm, pk_buf.at[0], local_sem.at[3]),
        pltpu.make_async_copy(pv_hbm, pv_buf.at[0], local_sem.at[4]),
    ]
    for copy in local:
        copy.start()
    order = [across_col for across_col in ((1 - y) * 2 + (1 - c), across, sibling, m)]
    w_copies = [
        pltpu.make_async_copy(
            w_hbm.at[:, pl.ds(pl.multiple_of(order[i] * width, 128), width)],
            w_buf.at[i],
            w_sem.at[i],
        )
        for i in range(4)
    ]
    for copy in w_copies:
        copy.start()
    pl.semaphore_wait(barrier, n + 1)

    def gather(k):
        pairs = (
            (meta_buf.at[0], meta_buf.at[k]),
            (k_hbm, k_buf.at[k]),
            (pk_hbm, pk_buf.at[k]),
            (v_hbm, v_buf.at[k]),
            (pv_hbm, pv_buf.at[k]),
        )
        return [
            pltpu.make_async_remote_copy(
                src_ref=source,
                dst_ref=target,
                send_sem=gather_send.at[k, i],
                recv_sem=gather_recv.at[k, i],
                device_id={"blk": peers[k]},
                device_id_type=MESH,
            )
            for i, (source, target) in enumerate(pairs)
        ]

    gathers = [None] + [gather(k) for k in range(1, n)]
    for i in range(5):
        for k in range(1, n):
            gathers[k][i].start()

    def column(row):
        return jnp.transpose(jnp.broadcast_to(row, (rows, rows)))

    query_row = deal_ref[...]
    start_row = jnp.zeros((1, rows), jnp.int32)
    group_row = jnp.full((1, rows), groups_ref[0], jnp.int32)
    end = lengths_ref[0]
    for r in range(1, requests):
        past = query_row >= end
        start_row = jnp.where(past, end, start_row)
        group_row = jnp.where(past, groups_ref[r], group_row)
        end = end + lengths_ref[r]
    row_col = column(query_row)
    start_col = column(start_row)
    group_col = column(group_row)

    for copy in local:
        copy.wait()
    scale = LOG2E / math.sqrt(HEAD_WIDTH)

    def scored(h, keys, bias):
        return (
            lax.dot_general(
                q_buf[:, h * HEAD_WIDTH : (h + 1) * HEAD_WIDTH],
                keys,
                (((1,), (1,)), ((), ())),
                preferred_element_type=jnp.float32,
            )
            * scale
            + bias
        )

    def place(block, keys, bias, first):
        for h in range(heads):
            scores = scored(h, keys, bias)
            score_buf[block, h] = scores
            if first:
                top_buf[h] = scores
            else:
                top_buf[h] = jnp.maximum(top_buf[h], scores)

    lane = lax.broadcasted_iota(jnp.int32, (1, rows), 1)
    for k in range(n):
        if k > 0:
            gathers[k][0].wait_recv()
            gathers[k][1].wait_recv()
        key_row = meta_buf[k, 0:1, :]
        shown = (key_row >= start_col) & (key_row <= row_col)
        bias = jnp.where(shown, 0.0, NEGATIVE)
        place(k, k_buf[k], bias, k == 0)
    for k in range(0, n, 2):
        for j in (k, k + 1):
            if j > 0:
                gathers[j][2].wait_recv()
        key_group = jnp.where(lane < rows // 2, meta_buf[k, 1:2, :], meta_buf[k + 1, 1:2, :])
        bias = jnp.where(key_group == group_col, 0.0, NEGATIVE)
        place(n + k // 2, pk_buf[k : k + 2].reshape(rows, HEAD_WIDTH), bias, False)

    blocks = n + n // 2
    totals = []
    for h in range(heads):
        top = jnp.max(top_buf[h], axis=1, keepdims=True)
        total = jnp.zeros((rows, rows), jnp.float32)
        for b in range(blocks):
            weights = jnp.exp2(score_buf[b, h] - top)
            total = total + weights
            weight_buf[h * rows : (h + 1) * rows, b * rows : (b + 1) * rows] = weights.astype(
                jnp.bfloat16
            )
        totals.append(jnp.sum(total, axis=1, keepdims=True))
    for k in range(1, n):
        gathers[k][3].wait_recv()
        gathers[k][4].wait_recv()
    mixed = jnp.dot(
        weight_buf[:, : n * rows],
        v_buf[...].reshape(n * rows, HEAD_WIDTH),
        preferred_element_type=jnp.float32,
    ) + jnp.dot(
        weight_buf[:, n * rows :],
        pv_buf[...].reshape(n * rows // 2, HEAD_WIDTH),
        preferred_element_type=jnp.float32,
    )
    for h in range(heads):
        done = (mixed[h * rows : (h + 1) * rows] / totals[h]).astype(jnp.bfloat16)
        att_buf[:, :, h * HEAD_WIDTH : (h + 1) * HEAD_WIDTH] = done.reshape(n, piece, HEAD_WIDTH)

    returns = [None] + [
        pltpu.make_async_remote_copy(
            src_ref=att_buf.at[peers[k]],
            dst_ref=ret_buf.at[k],
            send_sem=a2a_send.at[k],
            recv_sem=a2a_recv.at[k],
            device_id={"blk": peers[k]},
            device_id_type=MESH,
        )
        for k in range(1, n)
    ]
    for k in range(1, n):
        returns[k].start()
    ret_buf[0:1] = att_buf[pl.ds(me, 1)]

    placed = jnp.zeros((1, rows), jnp.int32)
    for k in range(n):
        shift = lax.rem((k + n - me) * piece, rows)
        turned = pltpu.roll(meta_buf[k], shift, 1)[0:1, :]
        placed = jnp.where((lane >= k * piece) & (lane < (k + 1) * piece), turned, placed)
    placed = placed - me * rows
    target = lax.broadcasted_iota(jnp.int32, (rows, rows), 0)
    select = jnp.where(target == placed, 1.0, 0.0).astype(jnp.bfloat16)
    for k in range(1, n):
        returns[k].wait_recv()
    ordered = jnp.dot(
        select, ret_buf[...].reshape(rows, -1), preferred_element_type=jnp.float32
    ).astype(jnp.bfloat16)

    def reduce_copy(i, source, target, device):
        return pltpu.make_async_remote_copy(
            src_ref=source,
            dst_ref=target,
            send_sem=red_send.at[i],
            recv_sem=red_recv.at[i],
            device_id={"mp": device},
            device_id_type=MESH,
        )

    def project(i):
        w_copies[i].wait()
        return jnp.dot(ordered, w_buf[i], preferred_element_type=jnp.float32)

    copy_a = reduce_copy(0, send_a, recv_a, sibling)
    copy_b = reduce_copy(1, send_b, recv_b, across)
    copy_c = reduce_copy(2, send_c, recv_c, sibling)
    send_a[...] = project(0).astype(jnp.bfloat16)
    copy_a.start()
    part_buf[...] = project(1)
    copy_a.wait_recv()
    send_b[...] = (part_buf[...] + recv_a[...].astype(jnp.float32)).astype(jnp.bfloat16)
    copy_b.start()
    send_c[...] = project(2).astype(jnp.bfloat16)
    copy_c.start()
    part_buf[...] = project(3)
    copy_c.wait_recv()
    part_buf[...] = part_buf[...] + recv_c[...].astype(jnp.float32)
    copy_b.wait_recv()
    out_ref[...] = (part_buf[...] + recv_b[...].astype(jnp.float32)).astype(jnp.bfloat16)
    for k in range(1, n):
        for copy in gathers[k]:
            copy.wait_send()
        returns[k].wait_send()
    for copy in (copy_a, copy_b, copy_c):
        copy.wait_send()


def shards(
    lengths,
    groups,
    deal,
    prefix_block,
    queries,
    keys,
    values,
    prefix_key_blocks,
    prefix_value_blocks,
    out_weight,
):
    n = lax.axis_size("blk")
    rows = queries.shape[0]
    piece = rows // n
    if piece % 16 != 0 or rows != 128 or 2 * prefix_key_blocks.shape[0] != rows:
        return plain_shards(
            lengths,
            groups,
            deal,
            prefix_block,
            queries,
            keys,
            values,
            prefix_key_blocks,
            prefix_value_blocks,
            out_weight,
        )
    heads = queries.shape[1] // HEAD_WIDTH
    prefix_rows = prefix_key_blocks.shape[0]
    columns = out_weight.shape[1] // lax.axis_size("mp")
    blocks = n + n // 2
    bf16, f32 = jnp.bfloat16, jnp.float32
    smem = pl.BlockSpec(memory_space=pltpu.SMEM)
    vmem = pl.BlockSpec(memory_space=pltpu.VMEM)
    hbm = pl.BlockSpec(memory_space=pl.ANY)
    dma = pltpu.SemaphoreType.DMA
    return pl.pallas_call(
        functools.partial(fused_kernel, n),
        out_shape=jax.ShapeDtypeStruct((rows, columns), bf16),
        in_specs=[smem, smem, smem, vmem, hbm, hbm, hbm, hbm, hbm, hbm],
        out_specs=vmem,
        scratch_shapes=[
            pltpu.VMEM((rows, queries.shape[1]), bf16),
            pltpu.VMEM((n, rows, HEAD_WIDTH), bf16),
            pltpu.VMEM((n, rows, HEAD_WIDTH), bf16),
            pltpu.VMEM((n, prefix_rows, HEAD_WIDTH), bf16),
            pltpu.VMEM((n, prefix_rows, HEAD_WIDTH), bf16),
            pltpu.VMEM((4, out_weight.shape[0], columns), bf16),
            pltpu.VMEM((n, 8, rows), jnp.int32),
            pltpu.VMEM((blocks, heads, rows, rows), f32),
            pltpu.VMEM((heads * rows, blocks * rows), bf16),
            pltpu.VMEM((heads, rows, rows), f32),
            pltpu.VMEM((rows, rows), f32),
            pltpu.VMEM((n, piece, heads * HEAD_WIDTH), bf16),
            pltpu.VMEM((n, piece, heads * HEAD_WIDTH), bf16),
        ]
        + [pltpu.VMEM((rows, columns), bf16)] * 6
        + [
            pltpu.VMEM((rows, columns), f32),
            dma((5,)),
            dma((1,)),
            dma((4,)),
            dma((n, 5)),
            dma((n, 5)),
            dma((n,)),
            dma((n,)),
            dma((3,)),
            dma((3,)),
        ],
        compiler_params=pltpu.CompilerParams(
            collective_id=0, has_side_effects=True, vmem_limit_bytes=40 << 20
        ),
    )(
        lengths,
        groups,
        prefix_block,
        deal.reshape(1, rows),
        queries,
        keys,
        values,
        prefix_key_blocks,
        prefix_value_blocks,
        out_weight,
    )


def solution(mesh):
    return jax.shard_map(
        shards,
        mesh=mesh,
        in_specs=(
            P(),
            P(),
            P("blk"),
            P("blk"),
            P("blk", "mp"),
            P("blk", "mp"),
            P("blk", "mp"),
            P("blk", "mp"),
            P("blk", "mp"),
            P("mp", None),
        ),
        out_specs=P("blk", "mp"),
        check_vma=False,
    )
```

```python
import functools
import math

import jax
import jax.numpy as jnp
from jax import lax
from jax.experimental import pallas as pl
from jax.experimental.pallas import tpu as pltpu
from jax.sharding import PartitionSpec as P

HEAD_WIDTH = 128
GROUPS = 4


NEGATIVE = -1e30


def request_index(row_ids, req_ends):
    return jnp.sum((row_ids[:, None] >= req_ends[None, :]).astype(jnp.int32), axis=1)


def lookup(values_table, indices):
    slots = jnp.arange(values_table.shape[0], dtype=jnp.int32)
    return jnp.sum(jnp.where(indices[:, None] == slots[None, :], values_table[None, :], 0), axis=1)


def attend(flash_state, grouped, key_block, value_block, visible):
    run_best, run_total, run_accum = flash_state
    key_count = key_block.shape[0]
    kv_heads = grouped.shape[1]
    head_size = grouped.shape[3]
    score_scale = 1.0 / math.sqrt(head_size)
    keys_three = key_block.reshape(key_count, kv_heads, head_size)
    values_three = value_block.reshape(key_count, kv_heads, head_size)
    scores = (
        jnp.einsum("rgjd,ngd->rgjn", grouped, keys_three, preferred_element_type=jnp.float32)
        * score_scale
    )
    shown = visible[:, None, None, :]
    scores = jnp.where(shown, scores, NEGATIVE)
    new_best = jnp.maximum(run_best, jnp.max(scores, axis=3))
    weights = jnp.where(shown, jnp.exp(scores - new_best[..., None]), 0.0)
    factor = jnp.exp(run_best - new_best)
    run_total = run_total * factor + jnp.sum(weights, axis=3)
    mixed = jnp.einsum(
        "rgjn,ngd->rgjd",
        weights.astype(jnp.bfloat16),
        values_three,
        preferred_element_type=jnp.float32,
    )
    run_accum = run_accum * factor[..., None] + mixed
    return (new_best, run_total, run_accum)


def sweep(flash_state, grouped, key_block, value_block, key_info, visible_of):
    key_count = key_block.shape[0]
    step_width = key_count if key_count <= 1024 else math.gcd(key_count, 512)
    if step_width == key_count:
        return attend(flash_state, grouped, key_block, value_block, visible_of(key_info))

    def one_step(carried, step_index):
        offset = step_index * step_width
        key_part = lax.dynamic_slice_in_dim(key_block, offset, step_width, 0)
        value_part = lax.dynamic_slice_in_dim(value_block, offset, step_width, 0)
        info_part = lax.dynamic_slice_in_dim(key_info, offset, step_width, 0)
        return (attend(carried, grouped, key_part, value_part, visible_of(info_part)), None)

    flash_state, _ = lax.scan(
        one_step, flash_state, jnp.arange(key_count // step_width, dtype=jnp.int32)
    )
    return flash_state


def plain_shards(
    lengths,
    groups,
    deal,
    prefix_block,
    queries,
    keys,
    values,
    prefix_key_blocks,
    prefix_value_blocks,
    out_weight,
):
    count_rows = queries.shape[0]
    kv_heads = keys.shape[1] // HEAD_WIDTH
    query_per_key_head = queries.shape[1] // keys.shape[1]
    devices = lax.axis_size("blk")
    my_index = lax.axis_index("blk")
    piece_rows = count_rows // devices
    per_group = devices // GROUPS
    prefix_rows = prefix_key_blocks.shape[0]
    req_ends = jnp.cumsum(lengths)
    arrived = lax.all_to_all(
        deal.reshape(devices, piece_rows), "blk", split_axis=0, concat_axis=0, tiled=True
    )
    placed = arrived.reshape(count_rows) - my_index * count_rows

    def prefix_pass(flash_state, grouped, query_group, block_ids):

        def prefix_step(carried, kv_piece):
            key_count = kv_piece[0].shape[0]
            owners = jnp.arange(key_count, dtype=jnp.int32) // prefix_rows
            key_group = jnp.take(block_ids, owners) // per_group

            def same_group(key_info):
                return key_info[None, :] == query_group[:, None]

            return sweep(carried, grouped, kv_piece[0], kv_piece[1], key_group, same_group)

        return prefix_step(
            flash_state,
            (
                lax.all_gather(prefix_key_blocks, "blk", axis=0, tiled=True),
                lax.all_gather(prefix_value_blocks, "blk", axis=0, tiled=True),
            ),
        )

    def suffix_rule(query_rows, query_req):

        def same_request(key_info):
            key_req = request_index(key_info, req_ends)
            return (
                (key_info[None, :] >= 0)
                & (key_req[None, :] == query_req[:, None])
                & (key_info[None, :] <= query_rows[:, None])
            )

        return same_request

    key_rows, block_ids = (
        lax.all_gather(deal, "blk", axis=0, tiled=True),
        lax.all_gather(prefix_block, "blk", axis=0, tiled=True),
    )
    query_rows = deal
    query_req = request_index(query_rows, req_ends)
    query_group = lookup(groups, query_req)
    grouped = queries.reshape(count_rows, kv_heads, query_per_key_head, HEAD_WIDTH)
    flash_state = prefix_pass(
        (
            jnp.full((count_rows, kv_heads, query_per_key_head), NEGATIVE, jnp.float32),
            jnp.zeros((count_rows, kv_heads, query_per_key_head), jnp.float32),
            jnp.zeros((count_rows, kv_heads, query_per_key_head, HEAD_WIDTH), jnp.float32),
        ),
        grouped,
        query_group,
        block_ids,
    )
    visible_of = suffix_rule(query_rows, query_req)
    kv_piece = (
        lax.all_gather(keys, "blk", axis=0, tiled=True),
        lax.all_gather(values, "blk", axis=0, tiled=True),
    )
    key_info = key_rows
    flash_state = sweep(flash_state, grouped, kv_piece[0], kv_piece[1], key_info, visible_of)
    run_best, run_total, run_accum = flash_state
    attended = (run_accum / run_total[..., None]).astype(jnp.bfloat16).reshape(count_rows, -1)
    returned = lax.all_to_all(
        attended.reshape(devices, piece_rows, -1), "blk", split_axis=0, concat_axis=0, tiled=True
    )
    flat = returned.reshape(count_rows, returned.shape[2])
    ordered = jnp.zeros_like(flat).at[placed].set(flat)
    partial_value = jnp.dot(ordered, out_weight, preferred_element_type=jnp.float32)
    return lax.psum_scatter(
        partial_value.astype(jnp.bfloat16), "mp", scatter_dimension=1, tiled=True
    )


LOG2E = 1.4426950408889634


def fused_kernel(
    devices,
    lengths_ref,
    groups_ref,
    block_ref,
    deal_ref,
    q_hbm,
    k_hbm,
    v_hbm,
    pk_hbm,
    pv_hbm,
    w_hbm,
    out_ref,
    q_buf,
    k_buf,
    v_buf,
    pk_buf,
    pv_buf,
    w_buf,
    meta_buf,
    score_buf,
    weight_buf,
    top_buf,
    bias_buf,
    att_buf,
    ret_buf,
    send_a,
    recv_a,
    send_b,
    recv_b,
    send_c,
    recv_c,
    part_buf,
    local_sem,
    own_sem,
    w_sem,
    gather_send,
    gather_recv,
    a2a_send,
    a2a_recv,
    red_send,
    red_recv,
):
    n = devices
    me = lax.axis_index("blk")
    m = lax.axis_index("mp")
    y = m // 2
    c = m - y * 2
    sibling = y * 2 + (1 - c)
    across = (1 - y) * 2 + c
    rows = q_buf.shape[0]
    heads = q_buf.shape[1] // HEAD_WIDTH
    piece = rows // n
    requests = lengths_ref.shape[0]
    per_group = n // GROUPS
    width = out_ref.shape[1]
    peers = [lax.rem(me + k, n) for k in range(n)]
    MESH = pl.DeviceIdType.MESH

    meta_buf[0] = jnp.zeros(meta_buf.shape[1:], jnp.int32)
    meta_buf[0, 0:1, :] = deal_ref[...]
    meta_buf[0, 1:2, :] = jnp.full((1, rows), block_ref[0] // per_group, jnp.int32)

    barrier = pltpu.get_barrier_semaphore()
    for k in range(1, n):
        pl.semaphore_signal(barrier, inc=1, device_id={"blk": peers[k]}, device_id_type=MESH)
    pl.semaphore_signal(barrier, inc=1, device_id={"mp": sibling}, device_id_type=MESH)
    pl.semaphore_signal(barrier, inc=1, device_id={"mp": across}, device_id_type=MESH)

    local = [
        pltpu.make_async_copy(q_hbm, q_buf, local_sem.at[0]),
        pltpu.make_async_copy(k_hbm, k_buf.at[0], local_sem.at[1]),
        pltpu.make_async_copy(v_hbm, v_buf.at[0], local_sem.at[2]),
        pltpu.make_async_copy(pk_hbm, pk_buf.at[0], local_sem.at[3]),
        pltpu.make_async_copy(pv_hbm, pv_buf.at[0], local_sem.at[4]),
    ]
    for copy in local:
        copy.start()
    order = [across_col for across_col in ((1 - y) * 2 + (1 - c), across, sibling, m)]
    w_copies = [
        pltpu.make_async_copy(
            w_hbm.at[:, pl.ds(pl.multiple_of(order[i] * width, 128), width)],
            w_buf.at[i],
            w_sem.at[i],
        )
        for i in range(4)
    ]
    for copy in w_copies:
        copy.start()
    pl.semaphore_wait(barrier, n + 1)

    def gather(k):
        pairs = (
            (meta_buf.at[0], meta_buf.at[k]),
            (k_hbm, k_buf.at[k]),
            (pk_hbm, pk_buf.at[k]),
            (v_hbm, v_buf.at[k]),
            (pv_hbm, pv_buf.at[k]),
        )
        return [
            pltpu.make_async_remote_copy(
                src_ref=source,
                dst_ref=target,
                send_sem=gather_send.at[k, i],
                recv_sem=gather_recv.at[k, i],
                device_id={"blk": peers[k]},
                device_id_type=MESH,
            )
            for i, (source, target) in enumerate(pairs)
        ]

    gathers = [None] + [gather(k) for k in range(1, n)]
    for i in range(5):
        for k in range(1, n):
            gathers[k][i].start()

    def column(row):
        return jnp.transpose(jnp.broadcast_to(row, (rows, rows)))

    query_row = deal_ref[...]
    start_row = jnp.zeros((1, rows), jnp.int32)
    group_row = jnp.full((1, rows), groups_ref[0], jnp.int32)
    end = lengths_ref[0]
    for r in range(1, requests):
        past = query_row >= end
        start_row = jnp.where(past, end, start_row)
        group_row = jnp.where(past, groups_ref[r], group_row)
        end = end + lengths_ref[r]
    row_col = column(query_row)
    start_col = column(start_row)
    group_col = column(group_row)

    for copy in local:
        copy.wait()
    scale = LOG2E / math.sqrt(HEAD_WIDTH)

    def scored(h, keys, bias):
        return (
            lax.dot_general(
                q_buf[:, h * HEAD_WIDTH : (h + 1) * HEAD_WIDTH],
                keys,
                (((1,), (1,)), ((), ())),
                preferred_element_type=jnp.float32,
            )
            * scale
            + bias
        )

    def place(block, keys, bias, first):
        for h in range(heads):
            scores = scored(h, keys, bias)
            score_buf[block, h] = scores
            if first:
                top_buf[h] = scores
            else:
                top_buf[h] = jnp.maximum(top_buf[h], scores)

    lane = lax.broadcasted_iota(jnp.int32, (1, rows), 1)
    for k in range(n):
        if k > 0:
            gathers[k][0].wait_recv()
            gathers[k][1].wait_recv()
        key_row = meta_buf[k, 0:1, :]
        shown = (key_row >= start_col) & (key_row <= row_col)
        bias = jnp.where(shown, 0.0, NEGATIVE)
        place(k, k_buf[k], bias, k == 0)
    for k in range(0, n, 2):
        for j in (k, k + 1):
            if j > 0:
                gathers[j][2].wait_recv()
        key_group = jnp.where(lane < rows // 2, meta_buf[k, 1:2, :], meta_buf[k + 1, 1:2, :])
        bias = jnp.where(key_group == group_col, 0.0, NEGATIVE)
        place(n + k // 2, pk_buf[k : k + 2].reshape(rows, HEAD_WIDTH), bias, False)

    blocks = n + n // 2
    totals = []
    for h in range(heads):
        top = jnp.max(top_buf[h], axis=1, keepdims=True)
        total = jnp.zeros((rows, rows), jnp.float32)
        for b in range(blocks):
            weights = jnp.exp2(score_buf[b, h] - top)
            total = total + weights
            weight_buf[h * rows : (h + 1) * rows, b * rows : (b + 1) * rows] = weights.astype(
                jnp.bfloat16
            )
        totals.append(jnp.sum(total, axis=1, keepdims=True))
    for k in range(1, n):
        gathers[k][3].wait_recv()
        gathers[k][4].wait_recv()
    mixed = jnp.dot(
        weight_buf[:, : n * rows],
        v_buf[...].reshape(n * rows, HEAD_WIDTH),
        preferred_element_type=jnp.float32,
    ) + jnp.dot(
        weight_buf[:, n * rows :],
        pv_buf[...].reshape(n * rows // 2, HEAD_WIDTH),
        preferred_element_type=jnp.float32,
    )
    for h in range(heads):
        done = (mixed[h * rows : (h + 1) * rows] / totals[h]).astype(jnp.bfloat16)
        att_buf[:, :, h * HEAD_WIDTH : (h + 1) * HEAD_WIDTH] = done.reshape(n, piece, HEAD_WIDTH)

    returns = [None] + [
        pltpu.make_async_remote_copy(
            src_ref=att_buf.at[peers[k]],
            dst_ref=ret_buf.at[k],
            send_sem=a2a_send.at[k],
            recv_sem=a2a_recv.at[k],
            device_id={"blk": peers[k]},
            device_id_type=MESH,
        )
        for k in range(1, n)
    ]
    for k in range(1, n):
        returns[k].start()
    ret_buf[0:1] = att_buf[pl.ds(me, 1)]

    placed = jnp.zeros((1, rows), jnp.int32)
    for k in range(n):
        shift = lax.rem((k + n - me) * piece, rows)
        turned = pltpu.roll(meta_buf[k], shift, 1)[0:1, :]
        placed = jnp.where((lane >= k * piece) & (lane < (k + 1) * piece), turned, placed)
    placed = placed - me * rows
    target = lax.broadcasted_iota(jnp.int32, (rows, rows), 0)
    select = jnp.where(target == placed, 1.0, 0.0).astype(jnp.bfloat16)
    for k in range(1, n):
        returns[k].wait_recv()
    ordered = jnp.dot(
        select, ret_buf[...].reshape(rows, -1), preferred_element_type=jnp.float32
    ).astype(jnp.bfloat16)

    def reduce_copy(i, source, target, device):
        return pltpu.make_async_remote_copy(
            src_ref=source,
            dst_ref=target,
            send_sem=red_send.at[i],
            recv_sem=red_recv.at[i],
            device_id={"mp": device},
            device_id_type=MESH,
        )

    def project(i):
        w_copies[i].wait()
        return jnp.dot(ordered, w_buf[i], preferred_element_type=jnp.float32)

    copy_a = reduce_copy(0, send_a, recv_a, sibling)
    copy_b = reduce_copy(1, send_b, recv_b, across)
    copy_c = reduce_copy(2, send_c, recv_c, sibling)
    send_a[...] = project(0).astype(jnp.bfloat16)
    copy_a.start()
    part_buf[...] = project(1)
    copy_a.wait_recv()
    send_b[...] = (part_buf[...] + recv_a[...].astype(jnp.float32)).astype(jnp.bfloat16)
    copy_b.start()
    send_c[...] = project(2).astype(jnp.bfloat16)
    copy_c.start()
    part_buf[...] = project(3)
    copy_c.wait_recv()
    part_buf[...] = part_buf[...] + recv_c[...].astype(jnp.float32)
    copy_b.wait_recv()
    out_ref[...] = (part_buf[...] + recv_b[...].astype(jnp.float32)).astype(jnp.bfloat16)
    for k in range(1, n):
        for copy in gathers[k]:
            copy.wait_send()
        returns[k].wait_send()
    for copy in (copy_a, copy_b, copy_c):
        copy.wait_send()


def shards(
    lengths,
    groups,
    deal,
    prefix_block,
    queries,
    keys,
    values,
    prefix_key_blocks,
    prefix_value_blocks,
    out_weight,
):
    n = lax.axis_size("blk")
    rows = queries.shape[0]
    piece = rows // n
    if piece % 16 != 0 or rows != 128 or 2 * prefix_key_blocks.shape[0] != rows:
        return plain_shards(
            lengths,
            groups,
            deal,
            prefix_block,
            queries,
            keys,
            values,
            prefix_key_blocks,
            prefix_value_blocks,
            out_weight,
        )
    heads = queries.shape[1] // HEAD_WIDTH
    prefix_rows = prefix_key_blocks.shape[0]
    columns = out_weight.shape[1] // lax.axis_size("mp")
    blocks = n + n // 2
    bf16, f32 = jnp.bfloat16, jnp.float32
    smem = pl.BlockSpec(memory_space=pltpu.SMEM)
    vmem = pl.BlockSpec(memory_space=pltpu.VMEM)
    hbm = pl.BlockSpec(memory_space=pl.ANY)
    dma = pltpu.SemaphoreType.DMA
    return pl.pallas_call(
        functools.partial(fused_kernel, n),
        out_shape=jax.ShapeDtypeStruct((rows, columns), bf16),
        in_specs=[smem, smem, smem, vmem, hbm, hbm, hbm, hbm, hbm, hbm],
        out_specs=vmem,
        scratch_shapes=[
            pltpu.VMEM((rows, queries.shape[1]), bf16),
            pltpu.VMEM((n, rows, HEAD_WIDTH), bf16),
            pltpu.VMEM((n, rows, HEAD_WIDTH), bf16),
            pltpu.VMEM((n, prefix_rows, HEAD_WIDTH), bf16),
            pltpu.VMEM((n, prefix_rows, HEAD_WIDTH), bf16),
            pltpu.VMEM((4, out_weight.shape[0], columns), bf16),
            pltpu.VMEM((n, 8, rows), jnp.int32),
            pltpu.VMEM((blocks, heads, rows, rows), f32),
            pltpu.VMEM((heads * rows, blocks * rows), bf16),
            pltpu.VMEM((heads, rows, rows), f32),
            pltpu.VMEM((rows, rows), f32),
            pltpu.VMEM((n, piece, heads * HEAD_WIDTH), bf16),
            pltpu.VMEM((n, piece, heads * HEAD_WIDTH), bf16),
        ]
        + [pltpu.VMEM((rows, columns), bf16)] * 6
        + [
            pltpu.VMEM((rows, columns), f32),
            dma((5,)),
            dma((1,)),
            dma((4,)),
            dma((n, 5)),
            dma((n, 5)),
            dma((n,)),
            dma((n,)),
            dma((3,)),
            dma((3,)),
        ],
        compiler_params=pltpu.CompilerParams(
            collective_id=0, has_side_effects=True, vmem_limit_bytes=60 << 20
        ),
    )(
        lengths,
        groups,
        prefix_block,
        deal.reshape(1, rows),
        queries,
        keys,
        values,
        prefix_key_blocks,
        prefix_value_blocks,
        out_weight,
    )


def solution(mesh):
    return jax.shard_map(
        shards,
        mesh=mesh,
        in_specs=(
            P(),
            P(),
            P("blk"),
            P("blk"),
            P("blk", "mp"),
            P("blk", "mp"),
            P("blk", "mp"),
            P("blk", "mp"),
            P("blk", "mp"),
            P("mp", None),
        ),
        out_specs=P("blk", "mp"),
        check_vma=False,
    )
```

```python
import functools
import math

import jax
import jax.numpy as jnp
from jax import lax
from jax.experimental import pallas as pl
from jax.experimental.pallas import tpu as pltpu
from jax.sharding import PartitionSpec as P

HEAD_WIDTH = 128
GROUPS = 4


NEGATIVE = -1e30


def request_index(row_ids, req_ends):
    return jnp.sum((row_ids[:, None] >= req_ends[None, :]).astype(jnp.int32), axis=1)


def lookup(values_table, indices):
    slots = jnp.arange(values_table.shape[0], dtype=jnp.int32)
    return jnp.sum(jnp.where(indices[:, None] == slots[None, :], values_table[None, :], 0), axis=1)


def attend(flash_state, grouped, key_block, value_block, visible):
    run_best, run_total, run_accum = flash_state
    key_count = key_block.shape[0]
    kv_heads = grouped.shape[1]
    head_size = grouped.shape[3]
    score_scale = 1.0 / math.sqrt(head_size)
    keys_three = key_block.reshape(key_count, kv_heads, head_size)
    values_three = value_block.reshape(key_count, kv_heads, head_size)
    scores = (
        jnp.einsum("rgjd,ngd->rgjn", grouped, keys_three, preferred_element_type=jnp.float32)
        * score_scale
    )
    shown = visible[:, None, None, :]
    scores = jnp.where(shown, scores, NEGATIVE)
    new_best = jnp.maximum(run_best, jnp.max(scores, axis=3))
    weights = jnp.where(shown, jnp.exp(scores - new_best[..., None]), 0.0)
    factor = jnp.exp(run_best - new_best)
    run_total = run_total * factor + jnp.sum(weights, axis=3)
    mixed = jnp.einsum(
        "rgjn,ngd->rgjd",
        weights.astype(jnp.bfloat16),
        values_three,
        preferred_element_type=jnp.float32,
    )
    run_accum = run_accum * factor[..., None] + mixed
    return (new_best, run_total, run_accum)


def sweep(flash_state, grouped, key_block, value_block, key_info, visible_of):
    key_count = key_block.shape[0]
    step_width = key_count if key_count <= 1024 else math.gcd(key_count, 512)
    if step_width == key_count:
        return attend(flash_state, grouped, key_block, value_block, visible_of(key_info))

    def one_step(carried, step_index):
        offset = step_index * step_width
        key_part = lax.dynamic_slice_in_dim(key_block, offset, step_width, 0)
        value_part = lax.dynamic_slice_in_dim(value_block, offset, step_width, 0)
        info_part = lax.dynamic_slice_in_dim(key_info, offset, step_width, 0)
        return (attend(carried, grouped, key_part, value_part, visible_of(info_part)), None)

    flash_state, _ = lax.scan(
        one_step, flash_state, jnp.arange(key_count // step_width, dtype=jnp.int32)
    )
    return flash_state


def plain_shards(
    lengths,
    groups,
    deal,
    prefix_block,
    queries,
    keys,
    values,
    prefix_key_blocks,
    prefix_value_blocks,
    out_weight,
):
    count_rows = queries.shape[0]
    kv_heads = keys.shape[1] // HEAD_WIDTH
    query_per_key_head = queries.shape[1] // keys.shape[1]
    devices = lax.axis_size("blk")
    my_index = lax.axis_index("blk")
    piece_rows = count_rows // devices
    per_group = devices // GROUPS
    prefix_rows = prefix_key_blocks.shape[0]
    req_ends = jnp.cumsum(lengths)
    arrived = lax.all_to_all(
        deal.reshape(devices, piece_rows), "blk", split_axis=0, concat_axis=0, tiled=True
    )
    placed = arrived.reshape(count_rows) - my_index * count_rows

    def prefix_pass(flash_state, grouped, query_group, block_ids):

        def prefix_step(carried, kv_piece):
            key_count = kv_piece[0].shape[0]
            owners = jnp.arange(key_count, dtype=jnp.int32) // prefix_rows
            key_group = jnp.take(block_ids, owners) // per_group

            def same_group(key_info):
                return key_info[None, :] == query_group[:, None]

            return sweep(carried, grouped, kv_piece[0], kv_piece[1], key_group, same_group)

        return prefix_step(
            flash_state,
            (
                lax.all_gather(prefix_key_blocks, "blk", axis=0, tiled=True),
                lax.all_gather(prefix_value_blocks, "blk", axis=0, tiled=True),
            ),
        )

    def suffix_rule(query_rows, query_req):

        def same_request(key_info):
            key_req = request_index(key_info, req_ends)
            return (
                (key_info[None, :] >= 0)
                & (key_req[None, :] == query_req[:, None])
                & (key_info[None, :] <= query_rows[:, None])
            )

        return same_request

    key_rows, block_ids = (
        lax.all_gather(deal, "blk", axis=0, tiled=True),
        lax.all_gather(prefix_block, "blk", axis=0, tiled=True),
    )
    query_rows = deal
    query_req = request_index(query_rows, req_ends)
    query_group = lookup(groups, query_req)
    grouped = queries.reshape(count_rows, kv_heads, query_per_key_head, HEAD_WIDTH)
    flash_state = prefix_pass(
        (
            jnp.full((count_rows, kv_heads, query_per_key_head), NEGATIVE, jnp.float32),
            jnp.zeros((count_rows, kv_heads, query_per_key_head), jnp.float32),
            jnp.zeros((count_rows, kv_heads, query_per_key_head, HEAD_WIDTH), jnp.float32),
        ),
        grouped,
        query_group,
        block_ids,
    )
    visible_of = suffix_rule(query_rows, query_req)
    kv_piece = (
        lax.all_gather(keys, "blk", axis=0, tiled=True),
        lax.all_gather(values, "blk", axis=0, tiled=True),
    )
    key_info = key_rows
    flash_state = sweep(flash_state, grouped, kv_piece[0], kv_piece[1], key_info, visible_of)
    run_best, run_total, run_accum = flash_state
    attended = (run_accum / run_total[..., None]).astype(jnp.bfloat16).reshape(count_rows, -1)
    returned = lax.all_to_all(
        attended.reshape(devices, piece_rows, -1), "blk", split_axis=0, concat_axis=0, tiled=True
    )
    flat = returned.reshape(count_rows, returned.shape[2])
    ordered = jnp.zeros_like(flat).at[placed].set(flat)
    partial_value = jnp.dot(ordered, out_weight, preferred_element_type=jnp.float32)
    return lax.psum_scatter(
        partial_value.astype(jnp.bfloat16), "mp", scatter_dimension=1, tiled=True
    )


LOG2E = 1.4426950408889634


def fused_kernel(
    devices,
    lengths_ref,
    groups_ref,
    block_ref,
    deal_ref,
    q_hbm,
    k_hbm,
    v_hbm,
    pk_hbm,
    pv_hbm,
    w_hbm,
    out_ref,
    q_buf,
    k_buf,
    v_buf,
    w_buf,
    meta_buf,
    col_buf,
    score_buf,
    weight_buf,
    top_buf,
    att_buf,
    send_a,
    recv_a,
    send_b,
    recv_b,
    send_c,
    recv_c,
    part_buf,
    local_sem,
    w_sem,
    up_send,
    down_send,
    cross_send,
    gather_recv,
    meta_send,
    meta_recv,
    a2a_send,
    a2a_recv,
    red_send,
    red_recv,
):
    n = devices
    me = lax.axis_index("blk")
    m = lax.axis_index("mp")
    y = m // 2
    c = m - y * 2
    sibling = y * 2 + (1 - c)
    across = (1 - y) * 2 + c
    rows = q_hbm.shape[0]
    heads = q_hbm.shape[1] // HEAD_WIDTH
    piece = rows // n
    requests = lengths_ref.shape[0]
    per_group = n // GROUPS
    width = out_ref.shape[1]
    lines = n // 2
    z = me // 2
    x = me - z * 2
    MESH = pl.DeviceIdType.MESH
    peers = [
        lax.rem(z + lines - s // 2, lines) * 2 + (x if s % 2 == 0 else 1 - x) for s in range(n)
    ]

    local = [
        pltpu.make_async_copy(k_hbm, k_buf.at[0, 0:rows], local_sem.at[0]),
        pltpu.make_async_copy(pk_hbm, k_buf.at[0, rows:], local_sem.at[1]),
        pltpu.make_async_copy(v_hbm, v_buf.at[0, 0:rows], local_sem.at[2]),
        pltpu.make_async_copy(pv_hbm, v_buf.at[0, rows:], local_sem.at[3]),
        pltpu.make_async_copy(
            q_hbm.at[pl.ds(pl.multiple_of(me * piece, piece), piece)],
            q_buf.at[0],
            local_sem.at[4],
        ),
    ]
    for copy in local:
        copy.start()
    meta_buf[0] = jnp.zeros(meta_buf.shape[1:], jnp.int32)
    meta_buf[0, 0:1, :] = deal_ref[...]
    meta_buf[0, 1:2, :] = jnp.full((1, rows), block_ref[0] // per_group, jnp.int32)

    barrier = pltpu.get_barrier_semaphore()
    for s in range(1, n):
        pl.semaphore_signal(barrier, inc=1, device_id={"blk": peers[s]}, device_id_type=MESH)
    pl.semaphore_signal(barrier, inc=1, device_id={"mp": sibling}, device_id_type=MESH)
    pl.semaphore_signal(barrier, inc=1, device_id={"mp": across}, device_id_type=MESH)
    order = [(1 - y) * 2 + (1 - c), across, sibling, m]
    w_copies = [
        pltpu.make_async_copy(
            w_hbm.at[:, pl.ds(pl.multiple_of(order[i] * width, 128), width)],
            w_buf.at[i],
            w_sem.at[i],
        )
        for i in range(4)
    ]
    for copy in local:
        copy.wait()
    for copy in w_copies:
        copy.start()
    pl.semaphore_wait(barrier, n + 1)

    bufs = (k_buf, v_buf)

    def hop(part, source, target, device, sem):
        return pltpu.make_async_remote_copy(
            src_ref=bufs[part].at[source],
            dst_ref=bufs[part].at[target],
            send_sem=sem.at[source // 2, part],
            recv_sem=gather_recv.at[target, part],
            device_id={"blk": device},
            device_id_type=MESH,
        )

    def up(part, r):
        return hop(part, 2 * r, 2 * ((r + lines - 1) % lines), me + 2, up_send)

    def down(part, r):
        return hop(part, 2 * r, 2 * ((r + 1) % lines), me - 2, down_send)

    def cross(part, r):
        return hop(part, 2 * r, 2 * r + 1, z * 2 + 1 - x, cross_send)

    def arrival(part, slot):
        return hop(part, 0, slot, z * 2 + 1 - x, cross_send)

    def forward(part, r, below, act):
        if below:

            @pl.when(z < lines - 1)
            def _():
                act(up(part, r))

        else:

            @pl.when(z > 0)
            def _():
                act(down(part, r))

        act(cross(part, r))

    def start(copy):
        copy.start()

    def ended(copy):
        copy.wait_send()

    queries_out = [None] + [
        pltpu.make_async_remote_copy(
            src_ref=q_hbm.at[pl.ds(pl.multiple_of(peers[s] * piece, piece), piece)],
            dst_ref=q_buf.at[s],
            send_sem=a2a_send.at[s],
            recv_sem=a2a_recv.at[s],
            device_id={"blk": peers[s]},
            device_id_type=MESH,
        )
        for s in range(1, n)
    ]
    metas_out = [None] + [
        pltpu.make_async_remote_copy(
            src_ref=meta_buf.at[0],
            dst_ref=meta_buf.at[s],
            send_sem=meta_send.at[s],
            recv_sem=meta_recv.at[s],
            device_id={"blk": peers[s]},
            device_id_type=MESH,
        )
        for s in range(1, n)
    ]

    def own(part, act):
        @pl.when(z < lines - 1)
        def _():
            act(up(part, 0))

        @pl.when(z > 0)
        def _():
            act(down(part, 0))

        act(cross(part, 0))

    own(0, start)
    for s in range(1, n):
        metas_out[s].start()
    for s in range(1, n):
        queries_out[s].start()
    own(1, start)

    def relay(distance):
        for part in range(2):
            for below in (True, False):
                r = lines - distance if below else distance

                @pl.when(z >= distance if below else z + distance < lines)
                def _(part=part, below=below, r=r):
                    arrival(part, 2 * r).wait_recv()
                    forward(part, r, below, start)

    def column(row):
        return jnp.transpose(jnp.broadcast_to(row, (rows, rows)))

    relay(1)
    lane = lax.broadcasted_iota(jnp.int32, (1, rows), 1)
    query_row = jnp.zeros((1, rows), jnp.int32)
    for s in range(n):
        if s > 0:
            metas_out[s].wait_recv()
        shift = lax.rem((s + n - me) * piece, rows)
        turned = pltpu.roll(meta_buf[s], shift, 1)[0:1, :]
        query_row = jnp.where((lane >= s * piece) & (lane < (s + 1) * piece), turned, query_row)
    target = lax.broadcasted_iota(jnp.int32, (rows, rows), 0)
    select = jnp.where(target == query_row - me * rows, 1.0, 0.0).astype(jnp.bfloat16)
    start_row = jnp.zeros((1, rows), jnp.int32)
    group_row = jnp.full((1, rows), groups_ref[0], jnp.int32)
    end = lengths_ref[0]
    for r in range(1, requests):
        past = query_row >= end
        start_row = jnp.where(past, end, start_row)
        group_row = jnp.where(past, groups_ref[r], group_row)
        end = end + lengths_ref[r]
    col_buf[0] = column(query_row)
    col_buf[1] = column(start_row)
    col_buf[2] = column(group_row)
    for s in range(1, n):
        queries_out[s].wait_recv()
    scale = LOG2E / math.sqrt(HEAD_WIDTH)

    def place(block, keys, bias, first):
        for h in range(heads):
            scores = (
                lax.dot_general(
                    q_buf[:, :, h * HEAD_WIDTH : (h + 1) * HEAD_WIDTH].reshape(rows, HEAD_WIDTH),
                    keys,
                    (((1,), (1,)), ((), ())),
                    preferred_element_type=jnp.float32,
                )
                * scale
                + bias
            )
            score_buf[block, h] = scores
            if first:
                top_buf[h] = scores
            else:
                top_buf[h] = jnp.maximum(top_buf[h], scores)

    def score_pair(r):
        arrival(0, 2 * r + 1).wait_recv()
        for s in (2 * r, 2 * r + 1):
            key_row = meta_buf[s, 0:1, :]
            shown = (key_row >= col_buf[1]) & (key_row <= col_buf[0])
            place(s, k_buf[s, 0:rows], jnp.where(shown, 0.0, NEGATIVE), s == 0)
        key_group = jnp.where(
            lane < rows // 2, meta_buf[2 * r, 1:2, :], meta_buf[2 * r + 1, 1:2, :]
        )
        bias = jnp.where(key_group == col_buf[2], 0.0, NEGATIVE)
        place(
            n + r, k_buf[2 * r : 2 * r + 2, rows:].reshape(rows, HEAD_WIDTH), bias, False
        )

    score_pair(0)
    for distance in range(1, lines):
        if distance + 1 < lines:
            relay(distance + 1)

        @pl.when(z >= distance)
        def _(r=lines - distance):
            score_pair(r)

        @pl.when(z + distance < lines)
        def _(r=distance):
            score_pair(r)

    blocks = n + n // 2
    totals = []
    for h in range(heads):
        top = jnp.max(top_buf[h], axis=1, keepdims=True)
        total = jnp.zeros((rows, rows), jnp.float32)
        for b in range(blocks):
            weights = jnp.exp2(score_buf[b, h] - top)
            total = total + weights
            weight_buf[h * rows : (h + 1) * rows, b * rows : (b + 1) * rows] = weights.astype(
                jnp.bfloat16
            )
        totals.append(jnp.sum(total, axis=1, keepdims=True))
    for r in range(lines):
        arrival(1, 2 * r + 1).wait_recv()
    mixed = jnp.dot(
        weight_buf[:, : n * rows],
        v_buf[:, 0:rows].reshape(n * rows, HEAD_WIDTH),
        preferred_element_type=jnp.float32,
    ) + jnp.dot(
        weight_buf[:, n * rows :],
        v_buf[:, rows:].reshape(n * rows // 2, HEAD_WIDTH),
        preferred_element_type=jnp.float32,
    )
    for h in range(heads):
        att_buf[:, h * HEAD_WIDTH : (h + 1) * HEAD_WIDTH] = (
            mixed[h * rows : (h + 1) * rows] / totals[h]
        ).astype(jnp.bfloat16)
    ordered = jnp.dot(select, att_buf[...], preferred_element_type=jnp.float32).astype(
        jnp.bfloat16
    )

    def reduce_copy(i, source, target, device):
        return pltpu.make_async_remote_copy(
            src_ref=source,
            dst_ref=target,
            send_sem=red_send.at[i],
            recv_sem=red_recv.at[i],
            device_id={"mp": device},
            device_id_type=MESH,
        )

    def project(i):
        w_copies[i].wait()
        return jnp.dot(ordered, w_buf[i], preferred_element_type=jnp.float32)

    copy_a = reduce_copy(0, send_a, recv_a, sibling)
    copy_b = reduce_copy(1, send_b, recv_b, across)
    copy_c = reduce_copy(2, send_c, recv_c, sibling)
    send_a[...] = project(0).astype(jnp.bfloat16)
    copy_a.start()
    part_buf[...] = project(1)
    copy_a.wait_recv()
    send_b[...] = (part_buf[...] + recv_a[...].astype(jnp.float32)).astype(jnp.bfloat16)
    copy_b.start()
    send_c[...] = project(2).astype(jnp.bfloat16)
    copy_c.start()
    part_buf[...] = project(3)
    copy_c.wait_recv()
    part_buf[...] = part_buf[...] + recv_c[...].astype(jnp.float32)
    copy_b.wait_recv()
    out_ref[...] = (part_buf[...] + recv_b[...].astype(jnp.float32)).astype(jnp.bfloat16)
    for s in range(1, n):
        metas_out[s].wait_send()
        queries_out[s].wait_send()
    for part in range(2):
        own(part, ended)
        for distance in range(1, lines):

            @pl.when(z >= distance)
            def _(part=part, r=lines - distance):
                forward(part, r, True, ended)

            @pl.when(z + distance < lines)
            def _(part=part, r=distance):
                forward(part, r, False, ended)

    for copy in (copy_a, copy_b, copy_c):
        copy.wait_send()


def shards(
    lengths,
    groups,
    deal,
    prefix_block,
    queries,
    keys,
    values,
    prefix_key_blocks,
    prefix_value_blocks,
    out_weight,
):
    n = lax.axis_size("blk")
    rows = queries.shape[0]
    piece = rows // n
    if piece % 16 != 0 or rows != 128 or 2 * prefix_key_blocks.shape[0] != rows:
        return plain_shards(
            lengths,
            groups,
            deal,
            prefix_block,
            queries,
            keys,
            values,
            prefix_key_blocks,
            prefix_value_blocks,
            out_weight,
        )
    heads = queries.shape[1] // HEAD_WIDTH
    prefix_rows = prefix_key_blocks.shape[0]
    columns = out_weight.shape[1] // lax.axis_size("mp")
    blocks = n + n // 2
    bf16, f32 = jnp.bfloat16, jnp.float32
    smem = pl.BlockSpec(memory_space=pltpu.SMEM)
    vmem = pl.BlockSpec(memory_space=pltpu.VMEM)
    hbm = pl.BlockSpec(memory_space=pl.ANY)
    dma = pltpu.SemaphoreType.DMA
    return pl.pallas_call(
        functools.partial(fused_kernel, n),
        out_shape=jax.ShapeDtypeStruct((rows, columns), bf16),
        in_specs=[smem, smem, smem, vmem, hbm, hbm, hbm, hbm, hbm, hbm],
        out_specs=vmem,
        scratch_shapes=[
            pltpu.VMEM((n, piece, queries.shape[1]), bf16),
            pltpu.VMEM((n, rows + prefix_rows, HEAD_WIDTH), bf16),
            pltpu.VMEM((n, rows + prefix_rows, HEAD_WIDTH), bf16),
            pltpu.VMEM((4, out_weight.shape[0], columns), bf16),
            pltpu.VMEM((n, 8, rows), jnp.int32),
            pltpu.VMEM((3, rows, rows), jnp.int32),
            pltpu.VMEM((blocks, heads, rows, rows), f32),
            pltpu.VMEM((heads * rows, blocks * rows), bf16),
            pltpu.VMEM((heads, rows, rows), f32),
            pltpu.VMEM((rows, heads * HEAD_WIDTH), bf16),
        ]
        + [pltpu.VMEM((rows, columns), bf16)] * 6
        + [
            pltpu.VMEM((rows, columns), f32),
            dma((5,)),
            dma((4,)),
            dma((n // 2, 2)),
            dma((n // 2, 2)),
            dma((n // 2, 2)),
            dma((n, 2)),
            dma((n,)),
            dma((n,)),
            dma((n,)),
            dma((n,)),
            dma((3,)),
            dma((3,)),
        ],
        compiler_params=pltpu.CompilerParams(
            collective_id=0, has_side_effects=True, vmem_limit_bytes=60 << 20
        ),
    )(
        lengths,
        groups,
        prefix_block,
        deal.reshape(1, rows),
        queries,
        keys,
        values,
        prefix_key_blocks,
        prefix_value_blocks,
        out_weight,
    )


def solution(mesh):
    return jax.shard_map(
        shards,
        mesh=mesh,
        in_specs=(
            P(),
            P(),
            P("blk"),
            P("blk"),
            P("blk", "mp"),
            P("blk", "mp"),
            P("blk", "mp"),
            P("blk", "mp"),
            P("blk", "mp"),
            P("mp", None),
        ),
        out_specs=P("blk", "mp"),
        check_vma=False,
    )
```

```python
import functools
import math

import jax
import jax.numpy as jnp
from jax import lax
from jax.experimental import pallas as pl
from jax.experimental.pallas import tpu as pltpu
from jax.sharding import PartitionSpec as P

HEAD_WIDTH = 128
GROUPS = 4


NEGATIVE = -1e30


def request_index(row_ids, req_ends):
    return jnp.sum((row_ids[:, None] >= req_ends[None, :]).astype(jnp.int32), axis=1)


def lookup(values_table, indices):
    slots = jnp.arange(values_table.shape[0], dtype=jnp.int32)
    return jnp.sum(jnp.where(indices[:, None] == slots[None, :], values_table[None, :], 0), axis=1)


def attend(flash_state, grouped, key_block, value_block, visible):
    run_best, run_total, run_accum = flash_state
    key_count = key_block.shape[0]
    kv_heads = grouped.shape[1]
    head_size = grouped.shape[3]
    score_scale = 1.0 / math.sqrt(head_size)
    keys_three = key_block.reshape(key_count, kv_heads, head_size)
    values_three = value_block.reshape(key_count, kv_heads, head_size)
    scores = (
        jnp.einsum("rgjd,ngd->rgjn", grouped, keys_three, preferred_element_type=jnp.float32)
        * score_scale
    )
    shown = visible[:, None, None, :]
    scores = jnp.where(shown, scores, NEGATIVE)
    new_best = jnp.maximum(run_best, jnp.max(scores, axis=3))
    weights = jnp.where(shown, jnp.exp(scores - new_best[..., None]), 0.0)
    factor = jnp.exp(run_best - new_best)
    run_total = run_total * factor + jnp.sum(weights, axis=3)
    mixed = jnp.einsum(
        "rgjn,ngd->rgjd",
        weights.astype(jnp.bfloat16),
        values_three,
        preferred_element_type=jnp.float32,
    )
    run_accum = run_accum * factor[..., None] + mixed
    return (new_best, run_total, run_accum)


def sweep(flash_state, grouped, key_block, value_block, key_info, visible_of):
    key_count = key_block.shape[0]
    step_width = key_count if key_count <= 1024 else math.gcd(key_count, 512)
    if step_width == key_count:
        return attend(flash_state, grouped, key_block, value_block, visible_of(key_info))

    def one_step(carried, step_index):
        offset = step_index * step_width
        key_part = lax.dynamic_slice_in_dim(key_block, offset, step_width, 0)
        value_part = lax.dynamic_slice_in_dim(value_block, offset, step_width, 0)
        info_part = lax.dynamic_slice_in_dim(key_info, offset, step_width, 0)
        return (attend(carried, grouped, key_part, value_part, visible_of(info_part)), None)

    flash_state, _ = lax.scan(
        one_step, flash_state, jnp.arange(key_count // step_width, dtype=jnp.int32)
    )
    return flash_state


def plain_shards(
    lengths,
    groups,
    deal,
    prefix_block,
    queries,
    keys,
    values,
    prefix_key_blocks,
    prefix_value_blocks,
    out_weight,
):
    count_rows = queries.shape[0]
    kv_heads = keys.shape[1] // HEAD_WIDTH
    query_per_key_head = queries.shape[1] // keys.shape[1]
    devices = lax.axis_size("blk")
    my_index = lax.axis_index("blk")
    piece_rows = count_rows // devices
    per_group = devices // GROUPS
    prefix_rows = prefix_key_blocks.shape[0]
    req_ends = jnp.cumsum(lengths)
    arrived = lax.all_to_all(
        deal.reshape(devices, piece_rows), "blk", split_axis=0, concat_axis=0, tiled=True
    )
    placed = arrived.reshape(count_rows) - my_index * count_rows

    def prefix_pass(flash_state, grouped, query_group, block_ids):

        def prefix_step(carried, kv_piece):
            key_count = kv_piece[0].shape[0]
            owners = jnp.arange(key_count, dtype=jnp.int32) // prefix_rows
            key_group = jnp.take(block_ids, owners) // per_group

            def same_group(key_info):
                return key_info[None, :] == query_group[:, None]

            return sweep(carried, grouped, kv_piece[0], kv_piece[1], key_group, same_group)

        return prefix_step(
            flash_state,
            (
                lax.all_gather(prefix_key_blocks, "blk", axis=0, tiled=True),
                lax.all_gather(prefix_value_blocks, "blk", axis=0, tiled=True),
            ),
        )

    def suffix_rule(query_rows, query_req):

        def same_request(key_info):
            key_req = request_index(key_info, req_ends)
            return (
                (key_info[None, :] >= 0)
                & (key_req[None, :] == query_req[:, None])
                & (key_info[None, :] <= query_rows[:, None])
            )

        return same_request

    key_rows, block_ids = (
        lax.all_gather(deal, "blk", axis=0, tiled=True),
        lax.all_gather(prefix_block, "blk", axis=0, tiled=True),
    )
    query_rows = deal
    query_req = request_index(query_rows, req_ends)
    query_group = lookup(groups, query_req)
    grouped = queries.reshape(count_rows, kv_heads, query_per_key_head, HEAD_WIDTH)
    flash_state = prefix_pass(
        (
            jnp.full((count_rows, kv_heads, query_per_key_head), NEGATIVE, jnp.float32),
            jnp.zeros((count_rows, kv_heads, query_per_key_head), jnp.float32),
            jnp.zeros((count_rows, kv_heads, query_per_key_head, HEAD_WIDTH), jnp.float32),
        ),
        grouped,
        query_group,
        block_ids,
    )
    visible_of = suffix_rule(query_rows, query_req)
    kv_piece = (
        lax.all_gather(keys, "blk", axis=0, tiled=True),
        lax.all_gather(values, "blk", axis=0, tiled=True),
    )
    key_info = key_rows
    flash_state = sweep(flash_state, grouped, kv_piece[0], kv_piece[1], key_info, visible_of)
    run_best, run_total, run_accum = flash_state
    attended = (run_accum / run_total[..., None]).astype(jnp.bfloat16).reshape(count_rows, -1)
    returned = lax.all_to_all(
        attended.reshape(devices, piece_rows, -1), "blk", split_axis=0, concat_axis=0, tiled=True
    )
    flat = returned.reshape(count_rows, returned.shape[2])
    ordered = jnp.zeros_like(flat).at[placed].set(flat)
    partial_value = jnp.dot(ordered, out_weight, preferred_element_type=jnp.float32)
    return lax.psum_scatter(
        partial_value.astype(jnp.bfloat16), "mp", scatter_dimension=1, tiled=True
    )


LOG2E = 1.4426950408889634


def fused_kernel(
    devices,
    lengths_ref,
    groups_ref,
    block_ref,
    deal_ref,
    q_hbm,
    k_hbm,
    v_hbm,
    pk_hbm,
    pv_hbm,
    w_hbm,
    out_ref,
    q_buf,
    ordered_q,
    k_buf,
    v_buf,
    w_buf,
    meta_buf,
    col_buf,
    score_buf,
    weight_buf,
    top_buf,
    att_buf,
    send_a,
    recv_a,
    send_b,
    recv_b,
    send_c,
    recv_c,
    part_buf,
    local_sem,
    w_sem,
    up_send,
    down_send,
    cross_send,
    gather_recv,
    meta_send,
    meta_recv,
    a2a_send,
    a2a_recv,
    red_send,
    red_recv,
):
    n = devices
    me = lax.axis_index("blk")
    m = lax.axis_index("mp")
    y = m // 2
    c = m - y * 2
    sibling = y * 2 + (1 - c)
    across = (1 - y) * 2 + c
    rows = q_hbm.shape[0]
    heads = q_hbm.shape[1] // HEAD_WIDTH
    piece = rows // n
    requests = lengths_ref.shape[0]
    per_group = n // GROUPS
    width = out_ref.shape[1]
    lines = n // 2
    z = me // 2
    x = me - z * 2
    MESH = pl.DeviceIdType.MESH
    peers = [
        lax.rem(z + lines - s // 2, lines) * 2 + (x if s % 2 == 0 else 1 - x) for s in range(n)
    ]

    lead = 2 * piece
    rest = lead + pk_hbm.shape[0]
    held = rows + pk_hbm.shape[0]
    window = pl.ds(pl.multiple_of((z // (lines - 1)) * lead, lead), held - lead)
    local = [
        pltpu.make_async_copy(k_hbm.at[0:lead], k_buf.at[0, 0:lead], local_sem.at[0]),
        pltpu.make_async_copy(pk_hbm, k_buf.at[0, lead:rest], local_sem.at[1]),
        pltpu.make_async_copy(k_hbm.at[lead:], k_buf.at[0, rest:], local_sem.at[2]),
        pltpu.make_async_copy(v_hbm.at[0:lead], v_buf.at[0, 0:lead], local_sem.at[3]),
        pltpu.make_async_copy(pv_hbm, v_buf.at[0, lead:rest], local_sem.at[5]),
        pltpu.make_async_copy(v_hbm.at[lead:], v_buf.at[0, rest:], local_sem.at[6]),
        pltpu.make_async_copy(
            q_hbm.at[pl.ds(pl.multiple_of(me * piece, piece), piece)],
            q_buf.at[0],
            local_sem.at[4],
        ),
    ]
    for copy in local:
        copy.start()
    for s in range(1, n, 2):
        for buf in (k_buf, v_buf):
            buf[s, 0:lead] = jnp.zeros((lead, HEAD_WIDTH), jnp.bfloat16)
            buf[s, held - lead :] = jnp.zeros((lead, HEAD_WIDTH), jnp.bfloat16)
    meta_buf[0] = jnp.zeros(meta_buf.shape[1:], jnp.int32)
    meta_buf[0, 0:1, :] = deal_ref[...]
    meta_buf[0, 1:2, :] = jnp.full((1, rows), block_ref[0] // per_group, jnp.int32)

    barrier = pltpu.get_barrier_semaphore()
    for s in range(1, n):
        pl.semaphore_signal(barrier, inc=1, device_id={"blk": peers[s]}, device_id_type=MESH)
    pl.semaphore_signal(barrier, inc=1, device_id={"mp": sibling}, device_id_type=MESH)
    pl.semaphore_signal(barrier, inc=1, device_id={"mp": across}, device_id_type=MESH)
    order = [(1 - y) * 2 + (1 - c), across, sibling, m]
    w_copies = [
        pltpu.make_async_copy(
            w_hbm.at[:, pl.ds(pl.multiple_of(order[i] * width, 128), width)],
            w_buf.at[i],
            w_sem.at[i],
        )
        for i in range(4)
    ]
    for copy in local:
        copy.wait()
    for copy in w_copies:
        copy.start()
    row_ids = lax.broadcasted_iota(jnp.int32, (rows, rows), 0) + me * rows
    start_row = jnp.zeros((rows, rows), jnp.int32)
    group_row = jnp.full((rows, rows), groups_ref[0], jnp.int32)
    end = lengths_ref[0]
    for r in range(1, requests):
        past = row_ids >= end
        start_row = jnp.where(past, end, start_row)
        group_row = jnp.where(past, groups_ref[r], group_row)
        end = end + lengths_ref[r]
    col_buf[0] = row_ids
    col_buf[1] = start_row
    col_buf[2] = group_row
    pl.semaphore_wait(barrier, n + 1)

    bufs = (k_buf, v_buf)

    def hop(part, source, target, device, sem):
        source_ref, target_ref = bufs[part].at[source], bufs[part].at[target]
        if target % 2 == 1:
            source_ref, target_ref = bufs[part].at[source, window], bufs[part].at[target, window]
        return pltpu.make_async_remote_copy(
            src_ref=source_ref,
            dst_ref=target_ref,
            send_sem=sem.at[source // 2, part],
            recv_sem=gather_recv.at[target, part],
            device_id={"blk": device},
            device_id_type=MESH,
        )

    def up(part, r):
        return hop(part, 2 * r, 2 * ((r + lines - 1) % lines), me + 2, up_send)

    def down(part, r):
        return hop(part, 2 * r, 2 * ((r + 1) % lines), me - 2, down_send)

    def cross(part, r):
        return hop(part, 2 * r, 2 * r + 1, z * 2 + 1 - x, cross_send)

    def arrival(part, slot):
        return hop(part, 0, slot, z * 2 + 1 - x, cross_send)

    def forward(part, r, below, act):
        if below:

            @pl.when(z < lines - 1)
            def _():
                act(up(part, r))

        else:

            @pl.when(z > 0)
            def _():
                act(down(part, r))

        act(cross(part, r))

    def start(copy):
        copy.start()

    def ended(copy):
        copy.wait_send()

    queries_out = [None] + [
        pltpu.make_async_remote_copy(
            src_ref=q_hbm.at[pl.ds(pl.multiple_of(peers[s] * piece, piece), piece)],
            dst_ref=q_buf.at[s],
            send_sem=a2a_send.at[s],
            recv_sem=a2a_recv.at[s],
            device_id={"blk": peers[s]},
            device_id_type=MESH,
        )
        for s in range(1, n)
    ]
    metas_out = [None] + [
        pltpu.make_async_remote_copy(
            src_ref=meta_buf.at[0],
            dst_ref=meta_buf.at[s],
            send_sem=meta_send.at[s],
            recv_sem=meta_recv.at[s],
            device_id={"blk": peers[s]},
            device_id_type=MESH,
        )
        for s in range(1, n)
    ]

    def own(part, act):
        @pl.when(z < lines - 1)
        def _():
            act(up(part, 0))

        @pl.when(z > 0)
        def _():
            act(down(part, 0))

        act(cross(part, 0))

    own(0, start)
    for s in range(1, n):
        metas_out[s].start()
    for s in range(1, n):
        queries_out[s].start()
    own(1, start)

    def relay(distance):
        for part in range(2):
            for below in (True, False):
                r = lines - distance if below else distance

                @pl.when(z >= distance if below else z + distance < lines)
                def _(part=part, below=below, r=r):
                    arrival(part, 2 * r).wait_recv()
                    forward(part, r, below, start)

    relay(1)
    lane = lax.broadcasted_iota(jnp.int32, (1, rows), 1)
    query_row = jnp.zeros((1, rows), jnp.int32)
    for s in range(n):
        if s > 0:
            metas_out[s].wait_recv()
        shift = lax.rem((s + n - me) * piece, rows)
        turned = pltpu.roll(meta_buf[s], shift, 1)[0:1, :]
        query_row = jnp.where((lane >= s * piece) & (lane < (s + 1) * piece), turned, query_row)
    select = jnp.where(col_buf[0] == query_row, 1.0, 0.0).astype(jnp.bfloat16)
    for s in range(1, n):
        queries_out[s].wait_recv()
    ordered_q[...] = jnp.dot(
        select, q_buf[...].reshape(rows, -1), preferred_element_type=jnp.float32
    ).astype(jnp.bfloat16)
    scale = LOG2E / math.sqrt(HEAD_WIDTH)

    def place(block, keys, bias, first):
        for h in range(heads):
            scores = (
                lax.dot_general(
                    ordered_q[:, h * HEAD_WIDTH : (h + 1) * HEAD_WIDTH],
                    keys,
                    (((1,), (1,)), ((), ())),
                    preferred_element_type=jnp.float32,
                )
                * scale
                + bias
            )
            score_buf[block, h] = scores
            if first:
                top_buf[h] = scores
            else:
                top_buf[h] = jnp.maximum(top_buf[h], scores)

    def score_pair(r):
        arrival(0, 2 * r + 1).wait_recv()
        for s in (2 * r, 2 * r + 1):
            key_row = meta_buf[s, 0:1, :]
            shown = (key_row >= col_buf[1]) & (key_row <= col_buf[0])
            suffix = jnp.concatenate([k_buf[s, 0:lead], k_buf[s, rest:]], axis=0)
            place(s, suffix, jnp.where(shown, 0.0, NEGATIVE), s == 0)
        key_group = jnp.where(
            lane < rows // 2, meta_buf[2 * r, 1:2, :], meta_buf[2 * r + 1, 1:2, :]
        )
        bias = jnp.where(key_group == col_buf[2], 0.0, NEGATIVE)
        place(
            n + r, k_buf[2 * r : 2 * r + 2, lead:rest].reshape(rows, HEAD_WIDTH), bias, False
        )

    score_pair(0)
    for distance in range(1, lines):
        if distance + 1 < lines:
            relay(distance + 1)

        @pl.when(z >= distance)
        def _(r=lines - distance):
            score_pair(r)

        @pl.when(z + distance < lines)
        def _(r=distance):
            score_pair(r)

    blocks = n + n // 2
    half = rows // 2

    def attention(i):
        part = slice(i * half, (i + 1) * half)
        totals = []
        for h in range(heads):
            top = jnp.max(top_buf[h, part], axis=1, keepdims=True)
            total = jnp.zeros((half, rows), jnp.float32)
            for b in range(blocks):
                weights = jnp.exp2(score_buf[b, h, part] - top)
                total = total + weights
                weight_buf[i, h * half : (h + 1) * half, b * rows : (b + 1) * rows] = (
                    weights.astype(jnp.bfloat16)
                )
            totals.append(jnp.sum(total, axis=1, keepdims=True))
        if i == 0:
            for r in range(lines):
                arrival(1, 2 * r + 1).wait_recv()
        suffix = jnp.concatenate([v_buf[:, 0:lead], v_buf[:, rest:]], axis=1)
        mixed = jnp.dot(
            weight_buf[i, :, : n * rows],
            suffix.reshape(n * rows, HEAD_WIDTH),
            preferred_element_type=jnp.float32,
        ) + jnp.dot(
            weight_buf[i, :, n * rows :],
            v_buf[:, lead:rest].reshape(n * rows // 2, HEAD_WIDTH),
            preferred_element_type=jnp.float32,
        )
        for h in range(heads):
            att_buf[part, h * HEAD_WIDTH : (h + 1) * HEAD_WIDTH] = (
                mixed[h * half : (h + 1) * half] / totals[h]
            ).astype(jnp.bfloat16)

    def reduce_copy(i, source, target, device):
        return pltpu.make_async_remote_copy(
            src_ref=source,
            dst_ref=target,
            send_sem=red_send.at[i],
            recv_sem=red_recv.at[i],
            device_id={"mp": device},
            device_id_type=MESH,
        )

    def project(i, part):
        return jnp.dot(att_buf[part], w_buf[i], preferred_element_type=jnp.float32)

    halves = [slice(i * half, (i + 1) * half) for i in range(2)]
    copies_a = [
        reduce_copy(i, send_a.at[p], recv_a.at[p], sibling) for i, p in enumerate(halves)
    ]
    copies_b = [
        reduce_copy(2 + i, send_b.at[p], recv_b.at[p], across) for i, p in enumerate(halves)
    ]
    copy_c = reduce_copy(4, send_c, recv_c, sibling)
    for i, p in enumerate(halves):
        attention(i)
        if i == 0:
            w_copies[0].wait()
        send_a[p] = project(0, p).astype(jnp.bfloat16)
        copies_a[i].start()
        if i == 0:
            w_copies[1].wait()
        part_buf[p] = project(1, p)
        copies_a[i].wait_recv()
        send_b[p] = (part_buf[p] + recv_a[p].astype(jnp.float32)).astype(jnp.bfloat16)
        copies_b[i].start()
    w_copies[2].wait()
    send_c[...] = project(2, slice(0, rows)).astype(jnp.bfloat16)
    copy_c.start()
    w_copies[3].wait()
    part_buf[...] = project(3, slice(0, rows))
    copy_c.wait_recv()
    part_buf[...] = part_buf[...] + recv_c[...].astype(jnp.float32)
    for copy, p in zip(copies_b, halves):
        copy.wait_recv()
        out_ref[p] = (part_buf[p] + recv_b[p].astype(jnp.float32)).astype(jnp.bfloat16)
    for s in range(1, n):
        metas_out[s].wait_send()
        queries_out[s].wait_send()
    for part in range(2):
        own(part, ended)
        for distance in range(1, lines):

            @pl.when(z >= distance)
            def _(part=part, r=lines - distance):
                forward(part, r, True, ended)

            @pl.when(z + distance < lines)
            def _(part=part, r=distance):
                forward(part, r, False, ended)

    for copy in copies_a + copies_b + [copy_c]:
        copy.wait_send()


def shards(
    lengths,
    groups,
    deal,
    prefix_block,
    queries,
    keys,
    values,
    prefix_key_blocks,
    prefix_value_blocks,
    out_weight,
):
    n = lax.axis_size("blk")
    rows = queries.shape[0]
    piece = rows // n
    if n != 8 or rows != 128 or 2 * prefix_key_blocks.shape[0] != rows:
        return plain_shards(
            lengths,
            groups,
            deal,
            prefix_block,
            queries,
            keys,
            values,
            prefix_key_blocks,
            prefix_value_blocks,
            out_weight,
        )
    heads = queries.shape[1] // HEAD_WIDTH
    prefix_rows = prefix_key_blocks.shape[0]
    columns = out_weight.shape[1] // lax.axis_size("mp")
    blocks = n + n // 2
    bf16, f32 = jnp.bfloat16, jnp.float32
    smem = pl.BlockSpec(memory_space=pltpu.SMEM)
    vmem = pl.BlockSpec(memory_space=pltpu.VMEM)
    hbm = pl.BlockSpec(memory_space=pl.ANY)
    dma = pltpu.SemaphoreType.DMA
    return pl.pallas_call(
        functools.partial(fused_kernel, n),
        out_shape=jax.ShapeDtypeStruct((rows, columns), bf16),
        in_specs=[smem, smem, smem, vmem, hbm, hbm, hbm, hbm, hbm, hbm],
        out_specs=vmem,
        scratch_shapes=[
            pltpu.VMEM((n, piece, queries.shape[1]), bf16),
            pltpu.VMEM((rows, queries.shape[1]), bf16),
            pltpu.VMEM((n, rows + prefix_rows, HEAD_WIDTH), bf16),
            pltpu.VMEM((n, rows + prefix_rows, HEAD_WIDTH), bf16),
            pltpu.VMEM((4, out_weight.shape[0], columns), bf16),
            pltpu.VMEM((n, 8, rows), jnp.int32),
            pltpu.VMEM((3, rows, rows), jnp.int32),
            pltpu.VMEM((blocks, heads, rows, rows), f32),
            pltpu.VMEM((2, heads * rows // 2, blocks * rows), bf16),
            pltpu.VMEM((heads, rows, rows), f32),
            pltpu.VMEM((rows, heads * HEAD_WIDTH), bf16),
        ]
        + [pltpu.VMEM((rows, columns), bf16)] * 6
        + [
            pltpu.VMEM((rows, columns), f32),
            dma((7,)),
            dma((4,)),
            dma((n // 2, 2)),
            dma((n // 2, 2)),
            dma((n // 2, 2)),
            dma((n, 2)),
            dma((n,)),
            dma((n,)),
            dma((n,)),
            dma((n,)),
            dma((5,)),
            dma((5,)),
        ],
        compiler_params=pltpu.CompilerParams(
            collective_id=0, has_side_effects=True, vmem_limit_bytes=60 << 20
        ),
    )(
        lengths,
        groups,
        prefix_block,
        deal.reshape(1, rows),
        queries,
        keys,
        values,
        prefix_key_blocks,
        prefix_value_blocks,
        out_weight,
    )


def solution(mesh):
    return jax.shard_map(
        shards,
        mesh=mesh,
        in_specs=(
            P(),
            P(),
            P("blk"),
            P("blk"),
            P("blk", "mp"),
            P("blk", "mp"),
            P("blk", "mp"),
            P("blk", "mp"),
            P("blk", "mp"),
            P("mp", None),
        ),
        out_specs=P("blk", "mp"),
        check_vma=False,
    )
```

```python
import functools
import math

import jax
import jax.numpy as jnp
from jax import lax
from jax.experimental import pallas as pl
from jax.experimental.pallas import tpu as pltpu
from jax.sharding import PartitionSpec as P

HEAD_WIDTH = 128
GROUPS = 4


NEGATIVE = -1e30


def request_index(row_ids, req_ends):
    return jnp.sum((row_ids[:, None] >= req_ends[None, :]).astype(jnp.int32), axis=1)


def lookup(values_table, indices):
    slots = jnp.arange(values_table.shape[0], dtype=jnp.int32)
    return jnp.sum(jnp.where(indices[:, None] == slots[None, :], values_table[None, :], 0), axis=1)


def attend(flash_state, grouped, key_block, value_block, visible):
    run_best, run_total, run_accum = flash_state
    key_count = key_block.shape[0]
    kv_heads = grouped.shape[1]
    head_size = grouped.shape[3]
    score_scale = 1.0 / math.sqrt(head_size)
    keys_three = key_block.reshape(key_count, kv_heads, head_size)
    values_three = value_block.reshape(key_count, kv_heads, head_size)
    scores = (
        jnp.einsum("rgjd,ngd->rgjn", grouped, keys_three, preferred_element_type=jnp.float32)
        * score_scale
    )
    shown = visible[:, None, None, :]
    scores = jnp.where(shown, scores, NEGATIVE)
    new_best = jnp.maximum(run_best, jnp.max(scores, axis=3))
    weights = jnp.where(shown, jnp.exp(scores - new_best[..., None]), 0.0)
    factor = jnp.exp(run_best - new_best)
    run_total = run_total * factor + jnp.sum(weights, axis=3)
    mixed = jnp.einsum(
        "rgjn,ngd->rgjd",
        weights.astype(jnp.bfloat16),
        values_three,
        preferred_element_type=jnp.float32,
    )
    run_accum = run_accum * factor[..., None] + mixed
    return (new_best, run_total, run_accum)


def sweep(flash_state, grouped, key_block, value_block, key_info, visible_of):
    key_count = key_block.shape[0]
    step_width = key_count if key_count <= 1024 else math.gcd(key_count, 512)
    if step_width == key_count:
        return attend(flash_state, grouped, key_block, value_block, visible_of(key_info))

    def one_step(carried, step_index):
        offset = step_index * step_width
        key_part = lax.dynamic_slice_in_dim(key_block, offset, step_width, 0)
        value_part = lax.dynamic_slice_in_dim(value_block, offset, step_width, 0)
        info_part = lax.dynamic_slice_in_dim(key_info, offset, step_width, 0)
        return (attend(carried, grouped, key_part, value_part, visible_of(info_part)), None)

    flash_state, _ = lax.scan(
        one_step, flash_state, jnp.arange(key_count // step_width, dtype=jnp.int32)
    )
    return flash_state


def plain_shards(
    lengths,
    groups,
    deal,
    prefix_block,
    queries,
    keys,
    values,
    prefix_key_blocks,
    prefix_value_blocks,
    out_weight,
):
    count_rows = queries.shape[0]
    kv_heads = keys.shape[1] // HEAD_WIDTH
    query_per_key_head = queries.shape[1] // keys.shape[1]
    devices = lax.axis_size("blk")
    my_index = lax.axis_index("blk")
    piece_rows = count_rows // devices
    per_group = devices // GROUPS
    prefix_rows = prefix_key_blocks.shape[0]
    req_ends = jnp.cumsum(lengths)
    arrived = lax.all_to_all(
        deal.reshape(devices, piece_rows), "blk", split_axis=0, concat_axis=0, tiled=True
    )
    placed = arrived.reshape(count_rows) - my_index * count_rows

    def prefix_pass(flash_state, grouped, query_group, block_ids):

        def prefix_step(carried, kv_piece):
            key_count = kv_piece[0].shape[0]
            owners = jnp.arange(key_count, dtype=jnp.int32) // prefix_rows
            key_group = jnp.take(block_ids, owners) // per_group

            def same_group(key_info):
                return key_info[None, :] == query_group[:, None]

            return sweep(carried, grouped, kv_piece[0], kv_piece[1], key_group, same_group)

        return prefix_step(
            flash_state,
            (
                lax.all_gather(prefix_key_blocks, "blk", axis=0, tiled=True),
                lax.all_gather(prefix_value_blocks, "blk", axis=0, tiled=True),
            ),
        )

    def suffix_rule(query_rows, query_req):

        def same_request(key_info):
            key_req = request_index(key_info, req_ends)
            return (
                (key_info[None, :] >= 0)
                & (key_req[None, :] == query_req[:, None])
                & (key_info[None, :] <= query_rows[:, None])
            )

        return same_request

    key_rows, block_ids = (
        lax.all_gather(deal, "blk", axis=0, tiled=True),
        lax.all_gather(prefix_block, "blk", axis=0, tiled=True),
    )
    query_rows = deal
    query_req = request_index(query_rows, req_ends)
    query_group = lookup(groups, query_req)
    grouped = queries.reshape(count_rows, kv_heads, query_per_key_head, HEAD_WIDTH)
    flash_state = prefix_pass(
        (
            jnp.full((count_rows, kv_heads, query_per_key_head), NEGATIVE, jnp.float32),
            jnp.zeros((count_rows, kv_heads, query_per_key_head), jnp.float32),
            jnp.zeros((count_rows, kv_heads, query_per_key_head, HEAD_WIDTH), jnp.float32),
        ),
        grouped,
        query_group,
        block_ids,
    )
    visible_of = suffix_rule(query_rows, query_req)
    kv_piece = (
        lax.all_gather(keys, "blk", axis=0, tiled=True),
        lax.all_gather(values, "blk", axis=0, tiled=True),
    )
    key_info = key_rows
    flash_state = sweep(flash_state, grouped, kv_piece[0], kv_piece[1], key_info, visible_of)
    run_best, run_total, run_accum = flash_state
    attended = (run_accum / run_total[..., None]).astype(jnp.bfloat16).reshape(count_rows, -1)
    returned = lax.all_to_all(
        attended.reshape(devices, piece_rows, -1), "blk", split_axis=0, concat_axis=0, tiled=True
    )
    flat = returned.reshape(count_rows, returned.shape[2])
    ordered = jnp.zeros_like(flat).at[placed].set(flat)
    partial_value = jnp.dot(ordered, out_weight, preferred_element_type=jnp.float32)
    return lax.psum_scatter(
        partial_value.astype(jnp.bfloat16), "mp", scatter_dimension=1, tiled=True
    )


LOG2E = 1.4426950408889634


def fused_kernel(
    devices,
    lengths_ref,
    groups_ref,
    block_ref,
    deal_ref,
    q_hbm,
    k_hbm,
    v_hbm,
    pk_hbm,
    pv_hbm,
    w_hbm,
    out_ref,
    q_buf,
    ordered_q,
    k_buf,
    v_buf,
    w_buf,
    meta_buf,
    col_buf,
    score_buf,
    weight_buf,
    top_buf,
    att_buf,
    send_a,
    recv_a,
    send_b,
    recv_b,
    send_c,
    recv_c,
    part_buf,
    local_sem,
    w_sem,
    up_send,
    down_send,
    cross_send,
    gather_recv,
    meta_send,
    meta_recv,
    a2a_send,
    a2a_recv,
    red_send,
    red_recv,
):
    n = devices
    me = lax.axis_index("blk")
    m = lax.axis_index("mp")
    y = m // 2
    c = m - y * 2
    sibling = y * 2 + (1 - c)
    across = (1 - y) * 2 + c
    rows = q_hbm.shape[0]
    heads = q_hbm.shape[1] // HEAD_WIDTH
    piece = rows // n
    requests = lengths_ref.shape[0]
    per_group = n // GROUPS
    width = out_ref.shape[1]
    lines = n // 2
    z = me // 2
    x = me - z * 2
    MESH = pl.DeviceIdType.MESH
    peers = [
        lax.rem(z + lines - s // 2, lines) * 2 + (x if s % 2 == 0 else 1 - x) for s in range(n)
    ]

    lead = 3 * piece
    rest = lead + pk_hbm.shape[0]
    held = rows + pk_hbm.shape[0]

    def window(block):
        first = jnp.maximum(block - n // 2, 0) * piece
        return pl.ds(pl.multiple_of(first, piece), held - lead)

    local = [
        pltpu.make_async_copy(k_hbm.at[0:lead], k_buf.at[0, 0:lead], local_sem.at[0]),
        pltpu.make_async_copy(pk_hbm, k_buf.at[0, lead:rest], local_sem.at[1]),
        pltpu.make_async_copy(k_hbm.at[lead:], k_buf.at[0, rest:], local_sem.at[2]),
        pltpu.make_async_copy(v_hbm.at[0:lead], v_buf.at[0, 0:lead], local_sem.at[3]),
        pltpu.make_async_copy(pv_hbm, v_buf.at[0, lead:rest], local_sem.at[5]),
        pltpu.make_async_copy(v_hbm.at[lead:], v_buf.at[0, rest:], local_sem.at[6]),
        pltpu.make_async_copy(
            q_hbm.at[pl.ds(pl.multiple_of(me * piece, piece), piece)],
            q_buf.at[0],
            local_sem.at[4],
        ),
    ]
    for copy in local:
        copy.start()
    for s in range(1, n, 2):
        for buf in (k_buf, v_buf):
            buf[s, 0:lead] = jnp.zeros((lead, HEAD_WIDTH), jnp.bfloat16)
            buf[s, held - lead :] = jnp.zeros((lead, HEAD_WIDTH), jnp.bfloat16)
    meta_buf[0] = jnp.zeros(meta_buf.shape[1:], jnp.int32)
    meta_buf[0, 0:1, :] = deal_ref[...]
    meta_buf[0, 1:2, :] = jnp.full((1, rows), block_ref[0] // per_group, jnp.int32)

    barrier = pltpu.get_barrier_semaphore()
    for s in range(1, n):
        pl.semaphore_signal(barrier, inc=1, device_id={"blk": peers[s]}, device_id_type=MESH)
    pl.semaphore_signal(barrier, inc=1, device_id={"mp": sibling}, device_id_type=MESH)
    pl.semaphore_signal(barrier, inc=1, device_id={"mp": across}, device_id_type=MESH)
    order = [(1 - y) * 2 + (1 - c), across, sibling, m]
    w_copies = [
        pltpu.make_async_copy(
            w_hbm.at[:, pl.ds(pl.multiple_of(order[i] * width, 128), width)],
            w_buf.at[i],
            w_sem.at[i],
        )
        for i in range(4)
    ]
    for copy in local:
        copy.wait()
    for copy in w_copies:
        copy.start()
    row_ids = lax.broadcasted_iota(jnp.int32, (rows, rows), 0) + me * rows
    start_row = jnp.zeros((rows, rows), jnp.int32)
    group_row = jnp.full((rows, rows), groups_ref[0], jnp.int32)
    end = lengths_ref[0]
    for r in range(1, requests):
        past = row_ids >= end
        start_row = jnp.where(past, end, start_row)
        group_row = jnp.where(past, groups_ref[r], group_row)
        end = end + lengths_ref[r]
    col_buf[0] = row_ids
    col_buf[1] = start_row
    col_buf[2] = group_row
    pl.semaphore_wait(barrier, n + 1)

    bufs = (k_buf, v_buf)

    def hop(part, source, target, device, sem):
        source_ref, target_ref = bufs[part].at[source], bufs[part].at[target]
        if target % 2 == 1:
            seen = window(me if sem is None else device)
            source_ref, target_ref = bufs[part].at[source, seen], bufs[part].at[target, seen]
            sem = cross_send
        return pltpu.make_async_remote_copy(
            src_ref=source_ref,
            dst_ref=target_ref,
            send_sem=sem.at[source // 2, part],
            recv_sem=gather_recv.at[target, part],
            device_id={"blk": device},
            device_id_type=MESH,
        )

    def up(part, r):
        return hop(part, 2 * r, 2 * ((r + lines - 1) % lines), me + 2, up_send)

    def down(part, r):
        return hop(part, 2 * r, 2 * ((r + 1) % lines), me - 2, down_send)

    def cross(part, r):
        return hop(part, 2 * r, 2 * r + 1, z * 2 + 1 - x, cross_send)

    def arrival(part, slot):
        return hop(part, 0, slot, z * 2 + 1 - x, None if slot % 2 == 1 else cross_send)

    def forward(part, r, below, act):
        if below:

            @pl.when(z < lines - 1)
            def _():
                act(up(part, r))

        else:

            @pl.when(z > 0)
            def _():
                act(down(part, r))

        act(cross(part, r))

    def start(copy):
        copy.start()

    def ended(copy):
        copy.wait_send()

    queries_out = [None] + [
        pltpu.make_async_remote_copy(
            src_ref=q_hbm.at[pl.ds(pl.multiple_of(peers[s] * piece, piece), piece)],
            dst_ref=q_buf.at[s],
            send_sem=a2a_send.at[s],
            recv_sem=a2a_recv.at[s],
            device_id={"blk": peers[s]},
            device_id_type=MESH,
        )
        for s in range(1, n)
    ]
    metas_out = [None] + [
        pltpu.make_async_remote_copy(
            src_ref=meta_buf.at[0],
            dst_ref=meta_buf.at[s],
            send_sem=meta_send.at[s],
            recv_sem=meta_recv.at[s],
            device_id={"blk": peers[s]},
            device_id_type=MESH,
        )
        for s in range(1, n)
    ]

    def own(part, act):
        @pl.when(z < lines - 1)
        def _():
            act(up(part, 0))

        @pl.when(z > 0)
        def _():
            act(down(part, 0))

        act(cross(part, 0))

    own(0, start)
    own(1, start)
    for s in range(1, n):
        metas_out[s].start()
    for s in range(1, n):
        queries_out[s].start()

    def relay(distance):
        for part in range(2):
            for below in (True, False):
                r = lines - distance if below else distance

                @pl.when(z >= distance if below else z + distance < lines)
                def _(part=part, below=below, r=r):
                    arrival(part, 2 * r).wait_recv()
                    forward(part, r, below, start)

    relay(1)
    lane = lax.broadcasted_iota(jnp.int32, (1, rows), 1)
    query_row = jnp.zeros((1, rows), jnp.int32)
    for s in range(n):
        if s > 0:
            metas_out[s].wait_recv()
        shift = lax.rem((s + n - me) * piece, rows)
        turned = pltpu.roll(meta_buf[s], shift, 1)[0:1, :]
        query_row = jnp.where((lane >= s * piece) & (lane < (s + 1) * piece), turned, query_row)
    select = jnp.where(col_buf[0] == query_row, 1.0, 0.0).astype(jnp.bfloat16)
    for s in range(1, n):
        queries_out[s].wait_recv()
    ordered_q[...] = jnp.dot(
        select, q_buf[...].reshape(rows, -1), preferred_element_type=jnp.float32
    ).astype(jnp.bfloat16)
    scale = LOG2E / math.sqrt(HEAD_WIDTH)

    def place(block, keys, bias, first):
        for h in range(heads):
            scores = (
                lax.dot_general(
                    ordered_q[:, h * HEAD_WIDTH : (h + 1) * HEAD_WIDTH],
                    keys,
                    (((1,), (1,)), ((), ())),
                    preferred_element_type=jnp.float32,
                )
                * scale
                + bias
            )
            score_buf[block, h] = scores
            if first:
                top_buf[h] = scores
            else:
                top_buf[h] = jnp.maximum(top_buf[h], scores)

    def score_pair(r):
        arrival(0, 2 * r + 1).wait_recv()
        for s in (2 * r, 2 * r + 1):
            key_row = meta_buf[s, 0:1, :]
            shown = (key_row >= col_buf[1]) & (key_row <= col_buf[0])
            suffix = jnp.concatenate([k_buf[s, 0:lead], k_buf[s, rest:]], axis=0)
            place(s, suffix, jnp.where(shown, 0.0, NEGATIVE), s == 0)
        key_group = jnp.where(
            lane < rows // 2, meta_buf[2 * r, 1:2, :], meta_buf[2 * r + 1, 1:2, :]
        )
        bias = jnp.where(key_group == col_buf[2], 0.0, NEGATIVE)
        place(
            n + r, k_buf[2 * r : 2 * r + 2, lead:rest].reshape(rows, HEAD_WIDTH), bias, False
        )

    score_pair(0)
    for distance in range(1, lines):
        if distance + 1 < lines:
            relay(distance + 1)

        @pl.when(z >= distance)
        def _(r=lines - distance):
            score_pair(r)

        @pl.when(z + distance < lines)
        def _(r=distance):
            score_pair(r)

    blocks = n + n // 2
    half = rows // 2

    def attention(i):
        part = slice(i * half, (i + 1) * half)
        totals = []
        for h in range(heads):
            top = jnp.max(top_buf[h, part], axis=1, keepdims=True)
            total = jnp.zeros((half, rows), jnp.float32)
            for b in range(blocks):
                weights = jnp.exp2(score_buf[b, h, part] - top)
                total = total + weights
                weight_buf[i, h * half : (h + 1) * half, b * rows : (b + 1) * rows] = (
                    weights.astype(jnp.bfloat16)
                )
            totals.append(jnp.sum(total, axis=1, keepdims=True))
        if i == 0:
            for r in range(lines):
                arrival(1, 2 * r + 1).wait_recv()
        suffix = jnp.concatenate([v_buf[:, 0:lead], v_buf[:, rest:]], axis=1)
        mixed = jnp.dot(
            weight_buf[i, :, : n * rows],
            suffix.reshape(n * rows, HEAD_WIDTH),
            preferred_element_type=jnp.float32,
        ) + jnp.dot(
            weight_buf[i, :, n * rows :],
            v_buf[:, lead:rest].reshape(n * rows // 2, HEAD_WIDTH),
            preferred_element_type=jnp.float32,
        )
        for h in range(heads):
            att_buf[part, h * HEAD_WIDTH : (h + 1) * HEAD_WIDTH] = (
                mixed[h * half : (h + 1) * half] / totals[h]
            ).astype(jnp.bfloat16)

    def reduce_copy(i, source, target, device):
        return pltpu.make_async_remote_copy(
            src_ref=source,
            dst_ref=target,
            send_sem=red_send.at[i],
            recv_sem=red_recv.at[i],
            device_id={"mp": device},
            device_id_type=MESH,
        )

    def project(i, part):
        return jnp.dot(att_buf[part], w_buf[i], preferred_element_type=jnp.float32)

    halves = [slice(i * half, (i + 1) * half) for i in range(2)]
    copies_a = [
        reduce_copy(i, send_a.at[p], recv_a.at[p], sibling) for i, p in enumerate(halves)
    ]
    copies_b = [
        reduce_copy(2 + i, send_b.at[p], recv_b.at[p], across) for i, p in enumerate(halves)
    ]
    copy_c = reduce_copy(4, send_c, recv_c, sibling)
    for i, p in enumerate(halves):
        attention(i)
        if i == 0:
            w_copies[0].wait()
        send_a[p] = project(0, p).astype(jnp.bfloat16)
        copies_a[i].start()
        if i == 0:
            w_copies[1].wait()
        part_buf[p] = project(1, p)
        copies_a[i].wait_recv()
        send_b[p] = (part_buf[p] + recv_a[p].astype(jnp.float32)).astype(jnp.bfloat16)
        copies_b[i].start()
    w_copies[2].wait()
    send_c[...] = project(2, slice(0, rows)).astype(jnp.bfloat16)
    copy_c.start()
    w_copies[3].wait()
    part_buf[...] = project(3, slice(0, rows))
    copy_c.wait_recv()
    part_buf[...] = part_buf[...] + recv_c[...].astype(jnp.float32)
    for copy, p in zip(copies_b, halves):
        copy.wait_recv()
        out_ref[p] = (part_buf[p] + recv_b[p].astype(jnp.float32)).astype(jnp.bfloat16)
    for s in range(1, n):
        metas_out[s].wait_send()
        queries_out[s].wait_send()
    for part in range(2):
        own(part, ended)
        for distance in range(1, lines):

            @pl.when(z >= distance)
            def _(part=part, r=lines - distance):
                forward(part, r, True, ended)

            @pl.when(z + distance < lines)
            def _(part=part, r=distance):
                forward(part, r, False, ended)

    for copy in copies_a + copies_b + [copy_c]:
        copy.wait_send()


def shards(
    lengths,
    groups,
    deal,
    prefix_block,
    queries,
    keys,
    values,
    prefix_key_blocks,
    prefix_value_blocks,
    out_weight,
):
    n = lax.axis_size("blk")
    rows = queries.shape[0]
    piece = rows // n
    if n != 8 or rows != 128 or 2 * prefix_key_blocks.shape[0] != rows:
        return plain_shards(
            lengths,
            groups,
            deal,
            prefix_block,
            queries,
            keys,
            values,
            prefix_key_blocks,
            prefix_value_blocks,
            out_weight,
        )
    heads = queries.shape[1] // HEAD_WIDTH
    prefix_rows = prefix_key_blocks.shape[0]
    columns = out_weight.shape[1] // lax.axis_size("mp")
    blocks = n + n // 2
    bf16, f32 = jnp.bfloat16, jnp.float32
    smem = pl.BlockSpec(memory_space=pltpu.SMEM)
    vmem = pl.BlockSpec(memory_space=pltpu.VMEM)
    hbm = pl.BlockSpec(memory_space=pl.ANY)
    dma = pltpu.SemaphoreType.DMA
    return pl.pallas_call(
        functools.partial(fused_kernel, n),
        out_shape=jax.ShapeDtypeStruct((rows, columns), bf16),
        in_specs=[smem, smem, smem, vmem, hbm, hbm, hbm, hbm, hbm, hbm],
        out_specs=vmem,
        scratch_shapes=[
            pltpu.VMEM((n, piece, queries.shape[1]), bf16),
            pltpu.VMEM((rows, queries.shape[1]), bf16),
            pltpu.VMEM((n, rows + prefix_rows, HEAD_WIDTH), bf16),
            pltpu.VMEM((n, rows + prefix_rows, HEAD_WIDTH), bf16),
            pltpu.VMEM((4, out_weight.shape[0], columns), bf16),
            pltpu.VMEM((n, 8, rows), jnp.int32),
            pltpu.VMEM((3, rows, rows), jnp.int32),
            pltpu.VMEM((blocks, heads, rows, rows), f32),
            pltpu.VMEM((2, heads * rows // 2, blocks * rows), bf16),
            pltpu.VMEM((heads, rows, rows), f32),
            pltpu.VMEM((rows, heads * HEAD_WIDTH), bf16),
        ]
        + [pltpu.VMEM((rows, columns), bf16)] * 6
        + [
            pltpu.VMEM((rows, columns), f32),
            dma((7,)),
            dma((4,)),
            dma((n // 2, 2)),
            dma((n // 2, 2)),
            dma((n // 2, 2)),
            dma((n, 2)),
            dma((n,)),
            dma((n,)),
            dma((n,)),
            dma((n,)),
            dma((5,)),
            dma((5,)),
        ],
        compiler_params=pltpu.CompilerParams(
            collective_id=0, has_side_effects=True, vmem_limit_bytes=60 << 20
        ),
    )(
        lengths,
        groups,
        prefix_block,
        deal.reshape(1, rows),
        queries,
        keys,
        values,
        prefix_key_blocks,
        prefix_value_blocks,
        out_weight,
    )


def solution(mesh):
    return jax.shard_map(
        shards,
        mesh=mesh,
        in_specs=(
            P(),
            P(),
            P("blk"),
            P("blk"),
            P("blk", "mp"),
            P("blk", "mp"),
            P("blk", "mp"),
            P("blk", "mp"),
            P("blk", "mp"),
            P("mp", None),
        ),
        out_specs=P("blk", "mp"),
        check_vma=False,
    )
```

```python
import functools
import math

import jax
import jax.numpy as jnp
from jax import lax
from jax.experimental import pallas as pl
from jax.experimental.pallas import tpu as pltpu
from jax.sharding import PartitionSpec as P

HEAD_WIDTH = 128
GROUPS = 4


NEGATIVE = -1e30


def request_index(row_ids, req_ends):
    return jnp.sum((row_ids[:, None] >= req_ends[None, :]).astype(jnp.int32), axis=1)


def lookup(values_table, indices):
    slots = jnp.arange(values_table.shape[0], dtype=jnp.int32)
    return jnp.sum(jnp.where(indices[:, None] == slots[None, :], values_table[None, :], 0), axis=1)


def attend(flash_state, grouped, key_block, value_block, visible):
    run_best, run_total, run_accum = flash_state
    key_count = key_block.shape[0]
    kv_heads = grouped.shape[1]
    head_size = grouped.shape[3]
    score_scale = 1.0 / math.sqrt(head_size)
    keys_three = key_block.reshape(key_count, kv_heads, head_size)
    values_three = value_block.reshape(key_count, kv_heads, head_size)
    scores = (
        jnp.einsum("rgjd,ngd->rgjn", grouped, keys_three, preferred_element_type=jnp.float32)
        * score_scale
    )
    shown = visible[:, None, None, :]
    scores = jnp.where(shown, scores, NEGATIVE)
    new_best = jnp.maximum(run_best, jnp.max(scores, axis=3))
    weights = jnp.where(shown, jnp.exp(scores - new_best[..., None]), 0.0)
    factor = jnp.exp(run_best - new_best)
    run_total = run_total * factor + jnp.sum(weights, axis=3)
    mixed = jnp.einsum(
        "rgjn,ngd->rgjd",
        weights.astype(jnp.bfloat16),
        values_three,
        preferred_element_type=jnp.float32,
    )
    run_accum = run_accum * factor[..., None] + mixed
    return (new_best, run_total, run_accum)


def sweep(flash_state, grouped, key_block, value_block, key_info, visible_of):
    key_count = key_block.shape[0]
    step_width = key_count if key_count <= 1024 else math.gcd(key_count, 512)
    if step_width == key_count:
        return attend(flash_state, grouped, key_block, value_block, visible_of(key_info))

    def one_step(carried, step_index):
        offset = step_index * step_width
        key_part = lax.dynamic_slice_in_dim(key_block, offset, step_width, 0)
        value_part = lax.dynamic_slice_in_dim(value_block, offset, step_width, 0)
        info_part = lax.dynamic_slice_in_dim(key_info, offset, step_width, 0)
        return (attend(carried, grouped, key_part, value_part, visible_of(info_part)), None)

    flash_state, _ = lax.scan(
        one_step, flash_state, jnp.arange(key_count // step_width, dtype=jnp.int32)
    )
    return flash_state


def plain_shards(
    lengths,
    groups,
    deal,
    prefix_block,
    queries,
    keys,
    values,
    prefix_key_blocks,
    prefix_value_blocks,
    out_weight,
):
    count_rows = queries.shape[0]
    kv_heads = keys.shape[1] // HEAD_WIDTH
    query_per_key_head = queries.shape[1] // keys.shape[1]
    devices = lax.axis_size("blk")
    my_index = lax.axis_index("blk")
    piece_rows = count_rows // devices
    per_group = devices // GROUPS
    prefix_rows = prefix_key_blocks.shape[0]
    req_ends = jnp.cumsum(lengths)
    arrived = lax.all_to_all(
        deal.reshape(devices, piece_rows), "blk", split_axis=0, concat_axis=0, tiled=True
    )
    placed = arrived.reshape(count_rows) - my_index * count_rows

    def prefix_pass(flash_state, grouped, query_group, block_ids):

        def prefix_step(carried, kv_piece):
            key_count = kv_piece[0].shape[0]
            owners = jnp.arange(key_count, dtype=jnp.int32) // prefix_rows
            key_group = jnp.take(block_ids, owners) // per_group

            def same_group(key_info):
                return key_info[None, :] == query_group[:, None]

            return sweep(carried, grouped, kv_piece[0], kv_piece[1], key_group, same_group)

        return prefix_step(
            flash_state,
            (
                lax.all_gather(prefix_key_blocks, "blk", axis=0, tiled=True),
                lax.all_gather(prefix_value_blocks, "blk", axis=0, tiled=True),
            ),
        )

    def suffix_rule(query_rows, query_req):

        def same_request(key_info):
            key_req = request_index(key_info, req_ends)
            return (
                (key_info[None, :] >= 0)
                & (key_req[None, :] == query_req[:, None])
                & (key_info[None, :] <= query_rows[:, None])
            )

        return same_request

    key_rows, block_ids = (
        lax.all_gather(deal, "blk", axis=0, tiled=True),
        lax.all_gather(prefix_block, "blk", axis=0, tiled=True),
    )
    query_rows = deal
    query_req = request_index(query_rows, req_ends)
    query_group = lookup(groups, query_req)
    grouped = queries.reshape(count_rows, kv_heads, query_per_key_head, HEAD_WIDTH)
    flash_state = prefix_pass(
        (
            jnp.full((count_rows, kv_heads, query_per_key_head), NEGATIVE, jnp.float32),
            jnp.zeros((count_rows, kv_heads, query_per_key_head), jnp.float32),
            jnp.zeros((count_rows, kv_heads, query_per_key_head, HEAD_WIDTH), jnp.float32),
        ),
        grouped,
        query_group,
        block_ids,
    )
    visible_of = suffix_rule(query_rows, query_req)
    kv_piece = (
        lax.all_gather(keys, "blk", axis=0, tiled=True),
        lax.all_gather(values, "blk", axis=0, tiled=True),
    )
    key_info = key_rows
    flash_state = sweep(flash_state, grouped, kv_piece[0], kv_piece[1], key_info, visible_of)
    run_best, run_total, run_accum = flash_state
    attended = (run_accum / run_total[..., None]).astype(jnp.bfloat16).reshape(count_rows, -1)
    returned = lax.all_to_all(
        attended.reshape(devices, piece_rows, -1), "blk", split_axis=0, concat_axis=0, tiled=True
    )
    flat = returned.reshape(count_rows, returned.shape[2])
    ordered = jnp.zeros_like(flat).at[placed].set(flat)
    partial_value = jnp.dot(ordered, out_weight, preferred_element_type=jnp.float32)
    return lax.psum_scatter(
        partial_value.astype(jnp.bfloat16), "mp", scatter_dimension=1, tiled=True
    )


LOG2E = 1.4426950408889634


def fused_kernel(
    devices,
    lengths_ref,
    groups_ref,
    block_ref,
    deal_ref,
    q_hbm,
    k_hbm,
    v_hbm,
    pk_hbm,
    pv_hbm,
    w_hbm,
    out_ref,
    q_buf,
    ordered_q,
    k_buf,
    v_buf,
    w_buf,
    meta_buf,
    col_buf,
    score_buf,
    weight_buf,
    top_buf,
    att_buf,
    send_a,
    recv_a,
    send_b,
    recv_b,
    send_c,
    recv_c,
    part_buf,
    local_sem,
    w_sem,
    up_send,
    down_send,
    cross_send,
    gather_recv,
    meta_send,
    meta_recv,
    a2a_send,
    a2a_recv,
    red_send,
    red_recv,
):
    n = devices
    me = lax.axis_index("blk")
    m = lax.axis_index("mp")
    y = m // 2
    c = m - y * 2
    sibling = y * 2 + (1 - c)
    across = (1 - y) * 2 + c
    rows = q_hbm.shape[0]
    heads = q_hbm.shape[1] // HEAD_WIDTH
    piece = rows // n
    requests = lengths_ref.shape[0]
    per_group = n // GROUPS
    width = out_ref.shape[1]
    lines = n // 2
    z = me // 2
    x = me - z * 2
    MESH = pl.DeviceIdType.MESH
    peers = [
        lax.rem(z + lines - s // 2, lines) * 2 + (x if s % 2 == 0 else 1 - x) for s in range(n)
    ]

    lead = 3 * piece
    rest = lead + pk_hbm.shape[0]
    held = rows + pk_hbm.shape[0]

    def window(block):
        first = jnp.maximum(block - n // 2, 0) * piece
        return pl.ds(pl.multiple_of(first, piece), held - lead)

    local = [
        pltpu.make_async_copy(k_hbm.at[0:lead], k_buf.at[0, 0:lead], local_sem.at[0]),
        pltpu.make_async_copy(pk_hbm, k_buf.at[0, lead:rest], local_sem.at[1]),
        pltpu.make_async_copy(k_hbm.at[lead:], k_buf.at[0, rest:], local_sem.at[2]),
        pltpu.make_async_copy(v_hbm.at[0:lead], v_buf.at[0, 0:lead], local_sem.at[3]),
        pltpu.make_async_copy(pv_hbm, v_buf.at[0, lead:rest], local_sem.at[5]),
        pltpu.make_async_copy(v_hbm.at[lead:], v_buf.at[0, rest:], local_sem.at[6]),
        pltpu.make_async_copy(
            q_hbm.at[pl.ds(pl.multiple_of(me * piece, piece), piece)],
            q_buf.at[0],
            local_sem.at[4],
        ),
    ]
    for copy in local:
        copy.start()
    for s in range(1, n, 2):
        for buf in (k_buf, v_buf):
            buf[s, 0:lead] = jnp.zeros((lead, HEAD_WIDTH), jnp.bfloat16)
            buf[s, held - lead :] = jnp.zeros((lead, HEAD_WIDTH), jnp.bfloat16)
    meta_buf[0] = jnp.zeros(meta_buf.shape[1:], jnp.int32)
    meta_buf[0, 0:1, :] = deal_ref[...]
    meta_buf[0, 1:2, :] = jnp.full((1, rows), block_ref[0] // per_group, jnp.int32)

    barrier = pltpu.get_barrier_semaphore()
    for s in range(1, n):
        pl.semaphore_signal(barrier, inc=1, device_id={"blk": peers[s]}, device_id_type=MESH)
    pl.semaphore_signal(barrier, inc=1, device_id={"mp": sibling}, device_id_type=MESH)
    pl.semaphore_signal(barrier, inc=1, device_id={"mp": across}, device_id_type=MESH)
    order = [(1 - y) * 2 + (1 - c), across, sibling, m]
    w_copies = [
        pltpu.make_async_copy(
            w_hbm.at[:, pl.ds(pl.multiple_of(order[i] * width, 128), width)],
            w_buf.at[i],
            w_sem.at[i],
        )
        for i in range(4)
    ]
    for copy in local:
        copy.wait()
    for copy in w_copies:
        copy.start()
    row_ids = lax.broadcasted_iota(jnp.int32, (rows, rows), 0) + me * rows
    start_row = jnp.zeros((rows, rows), jnp.int32)
    group_row = jnp.full((rows, rows), groups_ref[0], jnp.int32)
    end = lengths_ref[0]
    for r in range(1, requests):
        past = row_ids >= end
        start_row = jnp.where(past, end, start_row)
        group_row = jnp.where(past, groups_ref[r], group_row)
        end = end + lengths_ref[r]
    col_buf[0] = row_ids
    col_buf[1] = start_row
    col_buf[2] = group_row
    pl.semaphore_wait(barrier, n + 1)

    bufs = (k_buf, v_buf)

    def hop(part, source, target, device, sem):
        source_ref, target_ref = bufs[part].at[source], bufs[part].at[target]
        if target % 2 == 1:
            seen = window(me if sem is None else device)
            source_ref, target_ref = bufs[part].at[source, seen], bufs[part].at[target, seen]
            sem = cross_send
        return pltpu.make_async_remote_copy(
            src_ref=source_ref,
            dst_ref=target_ref,
            send_sem=sem.at[source // 2, part],
            recv_sem=gather_recv.at[target, part],
            device_id={"blk": device},
            device_id_type=MESH,
        )

    def up(part, r):
        return hop(part, 2 * r, 2 * ((r + lines - 1) % lines), me + 2, up_send)

    def down(part, r):
        return hop(part, 2 * r, 2 * ((r + 1) % lines), me - 2, down_send)

    def cross(part, r):
        return hop(part, 2 * r, 2 * r + 1, z * 2 + 1 - x, cross_send)

    def arrival(part, slot):
        return hop(part, 0, slot, z * 2 + 1 - x, None if slot % 2 == 1 else cross_send)

    def forward(part, r, below, act):
        if below:

            @pl.when(z < lines - 1)
            def _():
                act(up(part, r))

        else:

            @pl.when(z > 0)
            def _():
                act(down(part, r))

        act(cross(part, r))

    def start(copy):
        copy.start()

    def ended(copy):
        copy.wait_send()

    queries_out = [None] + [
        pltpu.make_async_remote_copy(
            src_ref=q_hbm.at[pl.ds(pl.multiple_of(peers[s] * piece, piece), piece)],
            dst_ref=q_buf.at[s],
            send_sem=a2a_send.at[s],
            recv_sem=a2a_recv.at[s],
            device_id={"blk": peers[s]},
            device_id_type=MESH,
        )
        for s in range(1, n)
    ]
    metas_out = [None] + [
        pltpu.make_async_remote_copy(
            src_ref=meta_buf.at[0],
            dst_ref=meta_buf.at[s],
            send_sem=meta_send.at[s],
            recv_sem=meta_recv.at[s],
            device_id={"blk": peers[s]},
            device_id_type=MESH,
        )
        for s in range(1, n)
    ]

    def own(part, act):
        @pl.when(z < lines - 1)
        def _():
            act(up(part, 0))

        @pl.when(z > 0)
        def _():
            act(down(part, 0))

        act(cross(part, 0))

    own(0, start)
    own(1, start)
    for s in range(1, n):
        metas_out[s].start()
    for s in range(1, n):
        queries_out[s].start()

    def relay(distance):
        for part in range(2):
            for below in (True, False):
                r = lines - distance if below else distance

                @pl.when(z >= distance if below else z + distance < lines)
                def _(part=part, below=below, r=r):
                    arrival(part, 2 * r).wait_recv()
                    forward(part, r, below, start)

    relay(1)
    relay(2)
    lane = lax.broadcasted_iota(jnp.int32, (1, rows), 1)
    query_row = jnp.zeros((1, rows), jnp.int32)
    for s in range(n):
        if s > 0:
            metas_out[s].wait_recv()
        shift = lax.rem((s + n - me) * piece, rows)
        turned = pltpu.roll(meta_buf[s], shift, 1)[0:1, :]
        query_row = jnp.where((lane >= s * piece) & (lane < (s + 1) * piece), turned, query_row)
    select = jnp.where(col_buf[0] == query_row, 1.0, 0.0).astype(jnp.bfloat16)
    for s in range(1, n):
        queries_out[s].wait_recv()
    ordered_q[...] = jnp.dot(
        select, q_buf[...].reshape(rows, -1), preferred_element_type=jnp.float32
    ).astype(jnp.bfloat16)
    scale = LOG2E / math.sqrt(HEAD_WIDTH)

    def place(block, keys, bias, first):
        for h in range(heads):
            scores = (
                lax.dot_general(
                    ordered_q[:, h * HEAD_WIDTH : (h + 1) * HEAD_WIDTH],
                    keys,
                    (((1,), (1,)), ((), ())),
                    preferred_element_type=jnp.float32,
                )
                * scale
                + bias
            )
            score_buf[block, h] = scores
            if first:
                top_buf[h] = scores
            else:
                top_buf[h] = jnp.maximum(top_buf[h], scores)

    def score_pair(r):
        arrival(0, 2 * r + 1).wait_recv()
        for s in (2 * r, 2 * r + 1):
            key_row = meta_buf[s, 0:1, :]
            shown = (key_row >= col_buf[1]) & (key_row <= col_buf[0])
            suffix = jnp.concatenate([k_buf[s, 0:lead], k_buf[s, rest:]], axis=0)
            place(s, suffix, jnp.where(shown, 0.0, NEGATIVE), s == 0)
        key_group = jnp.where(
            lane < rows // 2, meta_buf[2 * r, 1:2, :], meta_buf[2 * r + 1, 1:2, :]
        )
        bias = jnp.where(key_group == col_buf[2], 0.0, NEGATIVE)
        place(
            n + r, k_buf[2 * r : 2 * r + 2, lead:rest].reshape(rows, HEAD_WIDTH), bias, False
        )

    score_pair(0)
    for distance in range(1, lines):
        if 2 < distance + 1 < lines:
            relay(distance + 1)

        @pl.when(z >= distance)
        def _(r=lines - distance):
            score_pair(r)

        @pl.when(z + distance < lines)
        def _(r=distance):
            score_pair(r)

    blocks = n + n // 2
    half = rows // 2

    def attention(i):
        part = slice(i * half, (i + 1) * half)
        totals = []
        for h in range(heads):
            top = jnp.max(top_buf[h, part], axis=1, keepdims=True)
            total = jnp.zeros((half, rows), jnp.float32)
            for b in range(blocks):
                weights = jnp.exp2(score_buf[b, h, part] - top)
                total = total + weights
                weight_buf[i, h * half : (h + 1) * half, b * rows : (b + 1) * rows] = (
                    weights.astype(jnp.bfloat16)
                )
            totals.append(jnp.sum(total, axis=1, keepdims=True))
        if i == 0:
            for r in range(lines):
                arrival(1, 2 * r + 1).wait_recv()
        suffix = jnp.concatenate([v_buf[:, 0:lead], v_buf[:, rest:]], axis=1)
        mixed = jnp.dot(
            weight_buf[i, :, : n * rows],
            suffix.reshape(n * rows, HEAD_WIDTH),
            preferred_element_type=jnp.float32,
        ) + jnp.dot(
            weight_buf[i, :, n * rows :],
            v_buf[:, lead:rest].reshape(n * rows // 2, HEAD_WIDTH),
            preferred_element_type=jnp.float32,
        )
        for h in range(heads):
            att_buf[part, h * HEAD_WIDTH : (h + 1) * HEAD_WIDTH] = (
                mixed[h * half : (h + 1) * half] / totals[h]
            ).astype(jnp.bfloat16)

    def reduce_copy(i, source, target, device):
        return pltpu.make_async_remote_copy(
            src_ref=source,
            dst_ref=target,
            send_sem=red_send.at[i],
            recv_sem=red_recv.at[i],
            device_id={"mp": device},
            device_id_type=MESH,
        )

    def project(i, part):
        return jnp.dot(att_buf[part], w_buf[i], preferred_element_type=jnp.float32)

    halves = [slice(i * half, (i + 1) * half) for i in range(2)]
    copies_a = [
        reduce_copy(i, send_a.at[p], recv_a.at[p], sibling) for i, p in enumerate(halves)
    ]
    copies_b = [
        reduce_copy(2 + i, send_b.at[p], recv_b.at[p], across) for i, p in enumerate(halves)
    ]
    copy_c = reduce_copy(4, send_c, recv_c, sibling)
    for i, p in enumerate(halves):
        attention(i)
        if i == 0:
            w_copies[0].wait()
        send_a[p] = project(0, p).astype(jnp.bfloat16)
        copies_a[i].start()
        if i == 0:
            w_copies[1].wait()
        part_buf[p] = project(1, p)
        copies_a[i].wait_recv()
        send_b[p] = (part_buf[p] + recv_a[p].astype(jnp.float32)).astype(jnp.bfloat16)
        copies_b[i].start()
    w_copies[2].wait()
    send_c[...] = project(2, slice(0, rows)).astype(jnp.bfloat16)
    copy_c.start()
    w_copies[3].wait()
    part_buf[...] = project(3, slice(0, rows))
    copy_c.wait_recv()
    part_buf[...] = part_buf[...] + recv_c[...].astype(jnp.float32)
    for copy, p in zip(copies_b, halves):
        copy.wait_recv()
        out_ref[p] = (part_buf[p] + recv_b[p].astype(jnp.float32)).astype(jnp.bfloat16)
    for s in range(1, n):
        metas_out[s].wait_send()
        queries_out[s].wait_send()
    for part in range(2):
        own(part, ended)
        for distance in range(1, lines):

            @pl.when(z >= distance)
            def _(part=part, r=lines - distance):
                forward(part, r, True, ended)

            @pl.when(z + distance < lines)
            def _(part=part, r=distance):
                forward(part, r, False, ended)

    for copy in copies_a + copies_b + [copy_c]:
        copy.wait_send()


def shards(
    lengths,
    groups,
    deal,
    prefix_block,
    queries,
    keys,
    values,
    prefix_key_blocks,
    prefix_value_blocks,
    out_weight,
):
    n = lax.axis_size("blk")
    rows = queries.shape[0]
    piece = rows // n
    if n != 8 or rows != 128 or 2 * prefix_key_blocks.shape[0] != rows:
        return plain_shards(
            lengths,
            groups,
            deal,
            prefix_block,
            queries,
            keys,
            values,
            prefix_key_blocks,
            prefix_value_blocks,
            out_weight,
        )
    heads = queries.shape[1] // HEAD_WIDTH
    prefix_rows = prefix_key_blocks.shape[0]
    columns = out_weight.shape[1] // lax.axis_size("mp")
    blocks = n + n // 2
    bf16, f32 = jnp.bfloat16, jnp.float32
    smem = pl.BlockSpec(memory_space=pltpu.SMEM)
    vmem = pl.BlockSpec(memory_space=pltpu.VMEM)
    hbm = pl.BlockSpec(memory_space=pl.ANY)
    dma = pltpu.SemaphoreType.DMA
    return pl.pallas_call(
        functools.partial(fused_kernel, n),
        out_shape=jax.ShapeDtypeStruct((rows, columns), bf16),
        in_specs=[smem, smem, smem, vmem, hbm, hbm, hbm, hbm, hbm, hbm],
        out_specs=vmem,
        scratch_shapes=[
            pltpu.VMEM((n, piece, queries.shape[1]), bf16),
            pltpu.VMEM((rows, queries.shape[1]), bf16),
            pltpu.VMEM((n, rows + prefix_rows, HEAD_WIDTH), bf16),
            pltpu.VMEM((n, rows + prefix_rows, HEAD_WIDTH), bf16),
            pltpu.VMEM((4, out_weight.shape[0], columns), bf16),
            pltpu.VMEM((n, 8, rows), jnp.int32),
            pltpu.VMEM((3, rows, rows), jnp.int32),
            pltpu.VMEM((blocks, heads, rows, rows), f32),
            pltpu.VMEM((2, heads * rows // 2, blocks * rows), bf16),
            pltpu.VMEM((heads, rows, rows), f32),
            pltpu.VMEM((rows, heads * HEAD_WIDTH), bf16),
        ]
        + [pltpu.VMEM((rows, columns), bf16)] * 6
        + [
            pltpu.VMEM((rows, columns), f32),
            dma((7,)),
            dma((4,)),
            dma((n // 2, 2)),
            dma((n // 2, 2)),
            dma((n // 2, 2)),
            dma((n, 2)),
            dma((n,)),
            dma((n,)),
            dma((n,)),
            dma((n,)),
            dma((5,)),
            dma((5,)),
        ],
        compiler_params=pltpu.CompilerParams(
            collective_id=0, has_side_effects=True, vmem_limit_bytes=60 << 20
        ),
    )(
        lengths,
        groups,
        prefix_block,
        deal.reshape(1, rows),
        queries,
        keys,
        values,
        prefix_key_blocks,
        prefix_value_blocks,
        out_weight,
    )


def solution(mesh):
    return jax.shard_map(
        shards,
        mesh=mesh,
        in_specs=(
            P(),
            P(),
            P("blk"),
            P("blk"),
            P("blk", "mp"),
            P("blk", "mp"),
            P("blk", "mp"),
            P("blk", "mp"),
            P("blk", "mp"),
            P("mp", None),
        ),
        out_specs=P("blk", "mp"),
        check_vma=False,
    )
```
